128 devices in a mesh: row: 8 (over x_lo, y), col: 16 (over x_hi, z, core).
Axes of the slice: x: 4 (x_hi: 2, x_lo: 2; x = x_hi * 2 + x_lo), y: 4, z: 4, core: 2. Of those that a mesh axis runs over, the one named last changes fastest.
Arguments:
- r_vector: bfloat16 [3072, 18432], P(('row', 'col')), may hold values from -100 to 100, as said below
- r_previous: bfloat16 [3072, 18432], P(('row', 'col')), may hold values from -100 to 100, as said below
- cycle_block: bfloat16 [18432, 18432], P('row', 'col'), may hold values from -0.046875 to 0.046875
- ladder_block: bfloat16 [48, 48, 48, 48], P(None, 'col', None, 'row'), may hold values from -0.125 to 0.125
- occ_energy: float32 [48], replicated, may hold values from -3 to -0.5
- vir_energy: float32 [384], replicated, may hold values from 0.3 to 4
- beta_previous: float32 [64], replicated, may hold values from 0.3 to 3
Outputs:
- next_vector: bfloat16 [3072, 18432], P(('row', 'col'))
- alpha_coef: float32 [64], replicated
- beta_coef: float32 [64], replicated
The draws below stay inside these ranges and needn't reach their ends.
Inputs may be any that keep to these rules, and one draw needn't show every extreme that they name: `r_vector`: real-valued amplitudes, rough from entry to entry. `r_previous`: real-valued amplitudes, rough from entry to entry.
All inputs are finite; a program needn't handle non-finite values.
Results may differ from the reference program's by a relative error of at most 0.001.
Values may be sent and summed in bfloat16 or wider, within the bound.
A program may use at most 128 MiB of HBM per device.

```python
import math
import jax
import jax.numpy as jnp
from jax import lax

O = 48
V = 384
NVEC = 64


def scaled_vector(key):
    key_base, key_rows, key_cols = jax.random.split(key, 3)
    row_count = NVEC * O
    col_count = O * V
    position = (jnp.arange(row_count) % O).astype(jnp.float32) / (O - 1)
    row_scale = jnp.exp(jnp.log(10.0) * jax.random.uniform(key_rows, (row_count,))) * jnp.exp(jnp.log(3.0) * position)
    col_scale = jnp.exp(jnp.log(10.0) * jax.random.uniform(key_cols, (col_count,)))
    base_draw = jnp.clip(jax.random.normal(key_base, (row_count, col_count)), -4.0, 4.0)
    return (base_draw * row_scale[:, None] * col_scale[None, :] / 12.0).astype(jnp.bfloat16)


def draw_r_vector(key, part):
    return scaled_vector(jax.random.fold_in(key, 11))


def draw_r_previous(key, part):
    return scaled_vector(jax.random.fold_in(key, 23))


def shard_levels(stream_key, extent, pieces, smallest, largest):
    def one(axis_at, shards_of):
        steps = jax.random.uniform(jax.random.fold_in(jax.random.fold_in(stream_key, 6), axis_at), (shards_of,), jnp.float32, smallest / len(pieces), largest / len(pieces))
        return jnp.repeat(jnp.exp(steps), extent[axis_at] // shards_of).reshape((-1,) + (1,) * (len(extent) - axis_at - 1))

    factor_of = one(*pieces[0])
    for cut in pieces[1:]:
        factor_of = factor_of * one(*cut)
    return factor_of


def noise(rng, dims, scale, reach, shards=(), kind=jnp.bfloat16):
    entries = jax.random.normal(rng, dims, jnp.float32) * scale
    if len(shards) > 0:
        entries = shard_levels(rng, dims, shards, -0.22, 0.18) * entries
    return jnp.clip(entries, min=-reach, max=reach).astype(kind)


def setup_inputs(seed: int = 0) -> dict:
    arg_keys = jax.random.split(jax.random.key(seed), 8)
    r_vector = draw_r_vector(jax.random.fold_in(arg_keys[7], 71), 0)
    r_previous = draw_r_previous(jax.random.fold_in(arg_keys[7], 71), 0)
    cycle_block = noise(arg_keys[2], (O * V, O * V), (O * V) ** -0.5, 0.046875, ((0, 8), (1, 16)))
    ladder_block = noise(arg_keys[3], (O, O, O, O), (O * O) ** -0.5, 0.125, ((1, 16), (3, 8)))
    occ_energy = jnp.clip(jax.random.uniform(arg_keys[4], (O,), jnp.float32, -3.0, -0.5), -3.0, -0.5)
    vir_energy = jnp.clip(jnp.exp(jax.random.uniform(arg_keys[5], (V,), jnp.float32, math.log(0.3), math.log(4.0))), 0.3, 4.0)
    beta_previous = jnp.clip(jnp.exp(jax.random.uniform(arg_keys[6], (NVEC,), jnp.float32, math.log(0.3), math.log(3.0))), 0.3, 3.0)
    return {"r_vector": r_vector, "r_previous": r_previous, "cycle_block": cycle_block, "ladder_block": ladder_block, "occ_energy": occ_energy, "vir_energy": vir_energy, "beta_previous": beta_previous}


def per_vector(values):
    return lax.optimization_barrier(jnp.sum(values.reshape(NVEC, -1), axis=1))

def reference(r_vector, r_previous, cycle_block, ladder_block, occ_energy, vir_energy, beta_previous):
    row_count = NVEC * O
    r_float = r_vector.astype(jnp.float32)
    prev_float = r_previous.astype(jnp.float32)
    cycle_part = jnp.dot(r_float, cycle_block.astype(jnp.float32), precision=lax.Precision.HIGHEST)
    cube = r_float.reshape(NVEC, O, O, V)
    ladder_part = jnp.einsum('ijpq,npqa->nija', ladder_block.astype(jnp.float32), cube, precision=lax.Precision.HIGHEST).reshape(row_count, O * V)
    diagonal = vir_energy[None, None, None, :] - occ_energy[None, :, None, None] - occ_energy[None, None, :, None]
    sigma_rows = cycle_part + ladder_part + (diagonal * cube).reshape(row_count, O * V)
    count_all = O * O * V
    rs_sum = per_vector(r_float * sigma_rows)
    rr_sum = per_vector(r_float * r_float)
    alpha_coef = rs_sum / count_all / (rr_sum / count_all + 1e-06)
    residual_vec = sigma_rows - jnp.repeat(alpha_coef, O)[:, None] * r_float - jnp.repeat(beta_previous, O)[:, None] * prev_float
    beta_coef = jnp.sqrt(per_vector(residual_vec * residual_vec) / count_all + 1e-06)
    next_vector = (residual_vec / jnp.repeat(beta_coef, O)[:, None]).astype(jnp.bfloat16)
    return (next_vector, alpha_coef, beta_coef)
```

```python
import functools

import jax
import jax.numpy as jnp
from jax import lax
from jax.experimental import pallas as pl
from jax.experimental.pallas import tpu as pltpu
from jax.sharding import PartitionSpec as P

O = 48
V = 384
NVEC = 64
COUNT = O * O * V
H = 1152
HALF = O // 2
MESH = pl.DeviceIdType.MESH
ORDER = ((0, 0), (0, 1), (0, 3), (1, 0), (0, 2), (1, 1), (1, 3), (1, 2))
FORWARD = {
    0: (("down", (0, 1), 1), ("up", (0, 1), 2), ("across", (0, 1), 3)),
    1: (("down", (0,), 4),),
    2: (("up", (1,), 4),),
    3: (("down", (0, 1), 5), ("up", (0, 1), 6)),
    4: (),
    5: (("down", (0,), 7),),
    6: (("up", (1,), 7),),
    7: (),
}
SLOT = {}
for _t in range(8):
    for _kind, _parts, _to in FORWARD[_t]:
        for _p in _parts:
            SLOT[(_t, _kind, _p)] = len(SLOT)
F32 = jnp.float32
BF16 = jnp.bfloat16


def kernel(
    r_ref, prev_hbm, c_hbm, w_ref, dcol_ref, occ_ref, bprev_ref,
    nxt_ref, g_ref,
    c_v, prev_v, sib, r48, ob, p, ra, tin, xin, sig, st_out, st_in,
    load_sem, sib_s, sib_r, pa_s, pa_r, ag_s, ag_r, hs_s, hs_r,
    a_s, a_r, b_s, b_r, x_s, x_r, f_s, f_r, st_s, st_r, g_s, g_r,
):
    row, col = lax.axis_index("row"), lax.axis_index("col")
    xl, y = row // 4, row % 4
    xh, z, core = col // 8, (col % 8) // 2, col % 2

    def dev(xl_=None, y_=None, xh_=None, z_=None, core_=None):
        a = xl if xl_ is None else xl_
        b = y if y_ is None else y_
        c = xh if xh_ is None else xh_
        d = z if z_ is None else z_
        e = core if core_ is None else core_
        return (a * 4 + b, c * 8 + d * 2 + e)

    def remote(src, dst, ssem, rsem, to):
        return pltpu.make_async_remote_copy(
            src_ref=src, dst_ref=dst, send_sem=ssem, recv_sem=rsem,
            device_id=to, device_id_type=MESH,
        )

    y1, y2, y3 = (y + 1) % 4, (y + 2) % 4, (y + 3) % 4
    up, down = dev(z_=(z + 1) % 4), dev(z_=(z + 3) % 4)
    across = dev(xh_=1 - xh)
    sibling = dev(core_=1 - core)
    target = {"up": up, "down": down, "across": across}

    load_c = pltpu.make_async_copy(c_hbm, c_v, load_sem.at[0])
    load_p = pltpu.make_async_copy(prev_hbm, prev_v, load_sem.at[1])
    load_c.start()
    load_p.start()

    barrier = pltpu.get_barrier_semaphore()
    for d in range(1, 8):
        pl.semaphore_signal(barrier, inc=1, device_id=((row + d) % 8, col), device_id_type=MESH)
    for d in range(1, 16):
        pl.semaphore_signal(barrier, inc=1, device_id=(row, (col + d) % 16), device_id_type=MESH)
    pl.semaphore_signal(barrier, inc=1, device_id=dev(xl_=1 - xl, xh_=1 - xh), device_id_type=MESH)
    pl.semaphore_wait(barrier, 23)

    def rel(d):
        yd, xd = (y + d % 4) % 4, (xl + d // 4) % 2
        return yd, xd

    def cols(yd, xd, half):
        return pl.ds(pl.multiple_of(((xd * 4 + yd) * 2 + half) * H, 128), H)

    rel_order = (6, 2, 5, 7, 1, 3, 4, 0)

    def swap(d):
        yd, xd = rel(d)
        return remote(r_ref.at[:, cols(yd, xd, 1 - core)], sib.at[d], sib_s.at[d], sib_r.at[d], sibling)

    blk0 = xh * 4 + z

    def exchange(d):
        yd, xd = rel(d)
        return remote(r48.at[d], ob.at[blk0, core, y, xl], pa_s.at[d], pa_r.at[d], dev(xl_=xd, y_=yd))

    for d in rel_order:
        swap(d).start()
    for d in rel_order:
        yd, xd = rel(d)
        swap(d).wait_recv()
        mine = r_ref[:, cols(yd, xd, core)].astype(F32)
        other = sib[d].astype(F32)
        first = jnp.where(core == 0, mine, other)
        second = jnp.where(core == 0, other, mine)
        both = jnp.concatenate([first, second], axis=0).astype(BF16)
        if d == 0:
            ob[blk0, core, y, xl] = both
        else:
            r48[d] = both
            exchange(d).start()

    def block_of(t):
        out_x, out_z = xh, z
        for k, (dx, dz) in enumerate(ORDER):
            out_x = jnp.where(t == k, (xh + dx) % 2, out_x)
            out_z = jnp.where(t == k, (z + dz) % 4, out_z)
        return out_x, out_z

    def forward(t, kind, part, to):
        dx, dz = ORDER[t]
        blk = ((xh + dx) % 2) * 4 + (z + dz) % 4
        piece = ob.at[blk, core, pl.ds(2 * part, 2)]
        return remote(piece, piece, ag_s.at[SLOT[(t, kind, part)]], ag_r.at[to, part], target[kind])

    def hand(t):
        bx, bz = block_of(t)
        piece = ob.at[bx * 4 + bz, core]
        return remote(piece, piece, hs_s.at[t], hs_r.at[t], sibling)

    def landed(t, part):
        bx, bz = block_of(t)
        piece = ob.at[bx * 4 + bz, core, pl.ds(2 * part, 2)]
        return remote(piece, piece, ag_s.at[0], ag_r.at[t, part], sibling)

    def sibling_landed(t):
        bx, bz = block_of(t)
        piece = ob.at[bx * 4 + bz, 1 - core]
        return remote(piece, piece, hs_s.at[t], hs_r.at[t], sibling)

    def first_hop(s, side):
        to = dev(y_=y1) if side == 0 else dev(y_=y3)
        return remote(p.at[s, y2, side], ra.at[s, side], a_s.at[s, side], a_r.at[s, side], to)

    def second_hop(s, side):
        yd = y1 if side == 0 else y3
        return remote(p.at[s, yd], tin.at[s, side], b_s.at[s, side], b_r.at[s, side], dev(y_=yd))

    def beside(s):
        return remote(p.at[s, y, 1 - xl], xin.at[s], x_s.at[s], x_r.at[s], dev(xl_=1 - xl))

    def home(s, core_to):
        bx, bz = block_of(s)
        return remote(
            p.at[s, y, xl, pl.ds(core_to * HALF, HALF)], sig.at[col],
            f_s.at[s, core_to], f_r.at[col], dev(xh_=bx, z_=bz, core_=core_to),
        )

    def home_sibling():
        return remote(
            p.at[0, y, xl, pl.ds(pl.multiple_of((1 - core) * HALF, 8), HALF)], sig.at[col],
            f_s.at[0, 0], f_r.at[col], sibling,
        )

    load_c.wait()

    def step(t, carry):
        @pl.when(t == 0)
        def _():
            for d in range(1, 8):
                exchange(d).wait_recv()

        @pl.when(jnp.logical_and(t > 0, t < 8))
        def _():
            landed(t, 0).wait_recv()
            landed(t, 1).wait_recv()

        for k in range(8):
            if FORWARD[k]:
                @pl.when(t == k)
                def _(k=k):
                    for kind, parts, to in FORWARD[k]:
                        for part in parts:
                            forward(k, kind, part, to).start()

        @pl.when(t < 8)
        def _():
            hand(t).start()
            sibling_landed(t).wait_recv()
            bx, bz = block_of(t)
            blk = bx * 4 + bz
            x0 = ob[blk, 0].reshape(8 * O, H)
            x1 = ob[blk, 1].reshape(8 * O, H)
            acc = jnp.dot(x0, c_v[:H], preferred_element_type=F32)
            acc = acc + jnp.dot(x1, c_v[H:], preferred_element_type=F32)
            p[t] = acc.reshape(4, 2, O, H)

            def ladder(v, carry2):
                vy, vx = v // 2, v % 2
                stack = jnp.concatenate(
                    [ob[blk, h, vy, vx, :, q * V:(q + 1) * V] for h in range(2) for q in range(3)],
                    axis=0,
                )
                part = jnp.dot(w_ref[...], stack, preferred_element_type=F32)
                for j in range(3):
                    p[t, vy, vx, :, j * V:(j + 1) * V] += part[j * O:(j + 1) * O]
                return carry2

            lax.fori_loop(0, 8, ladder, 0)
            first_hop(t, 0).start()
            first_hop(t, 1).start()

        @pl.when(jnp.logical_and(t >= 1, t <= 8))
        def _():
            s = t - 1
            first_hop(s, 0).wait_recv()
            p[s, y1, 0] += ra[s, 0]
            second_hop(s, 0).start()
            first_hop(s, 1).wait_recv()
            p[s, y3, 1] += ra[s, 1]
            second_hop(s, 1).start()

        @pl.when(jnp.logical_and(t >= 2, t <= 9))
        def _():
            s = t - 2
            second_hop(s, 0).wait_recv()
            second_hop(s, 1).wait_recv()
            p[s, y, 1 - xl] += tin[s, 0, 1 - xl] + tin[s, 1, 1 - xl]
            beside(s).start()
            p[s, y, xl] += tin[s, 0, xl] + tin[s, 1, xl]

        @pl.when(t >= 3)
        def _():
            s = t - 3
            beside(s).wait_recv()
            p[s, y, xl] += xin[s]

            @pl.when(s == 0)
            def _():
                home_sibling().start()
                sig[col] = p[0, y, xl, pl.ds(pl.multiple_of(core * HALF, 8), HALF)]

            @pl.when(s > 0)
            def _():
                home(s, 0).start()
                home(s, 1).start()

        return carry

    lax.fori_loop(0, 11, step, 0)
    load_p.wait()

    def sums(val):
        total = val[:, 0:128]
        for k in range(1, H // 128):
            total = total + val[:, k * 128:(k + 1) * 128]
        return total[0:8] + total[8:16] + total[16:24]

    occ_col = occ_ref[:, 0:1]

    def arrived(d):
        from_col = (col + d) % 16
        return remote(sig.at[from_col], sig.at[from_col], f_s.at[0, 0], f_r.at[from_col], sibling)

    def first_pass(d, carry):
        acc_s, acc_r = carry
        @pl.when(d > 0)
        def _():
            arrived(d).wait_recv()
        k = (col + d) % 16
        rv = r_ref[:, pl.ds(pl.multiple_of(k * H, 128), H)].astype(F32)
        val = sig[k] + (dcol_ref[k] - occ_col) * rv
        sig[k] = val
        return acc_s + sums(rv * val), acc_r + sums(rv * rv)

    zero = jnp.zeros((8, 128), F32)
    acc_s, acc_r = lax.fori_loop(0, 16, first_pass, (zero, zero))
    line = lax.broadcasted_iota(jnp.int32, (8, 128), 0)

    def pair(k):
        return remote(st_out.at[k], st_in.at[k], st_s.at[k], st_r.at[k], sibling)

    st_out[0] = jnp.where(line == 0, jnp.sum(acc_s), jnp.sum(acc_r))
    pair(0).start()
    pair(0).wait_recv()
    both = st_out[0] + st_in[0]
    alpha = both[0:1] / COUNT / (both[1:2] / COUNT + 1e-06)
    alpha_1 = alpha[:, 0:1]
    bprev_1 = bprev_ref[0:1, 0:1]

    def second_pass(k, acc):
        at = pl.ds(pl.multiple_of(k * H, 128), H)
        val = sig[k] - alpha_1 * r_ref[:, at].astype(F32) - bprev_1 * prev_v[:, at].astype(F32)
        sig[k] = val
        return acc + sums(val * val)

    acc_n = lax.fori_loop(0, 16, second_pass, zero)
    st_out[1] = jnp.where(line == 0, jnp.sum(acc_n), 0.0)
    pair(1).start()
    pair(1).wait_recv()
    norm = (st_out[1] + st_in[1])[0:1]
    beta = jnp.sqrt(norm / COUNT + 1e-06)
    inv = (1.0 / beta)[:, 0:1]

    g_ref[xl, y, xh, z] = jnp.where(line == 0, alpha, beta)

    def spread(axis, d):
        if axis == 0:
            piece, to = g_ref.at[xl, y, xh, z], dev(z_=(z + d) % 4)
        elif axis == 1:
            piece, to = g_ref.at[xl, y, xh], dev(y_=(y + d) % 4)
        else:
            piece = g_ref.at[xl, :, xh]
            to = dev(xl_=(xl + d % 2) % 2, xh_=(xh + d // 2) % 2)
        return remote(piece, piece, g_s.at[axis, d - 1], g_r.at[axis, d - 1], to)

    for d in range(1, 4):
        spread(0, d).start()

    def third_pass(k, carry):
        nxt_ref[:, pl.ds(pl.multiple_of(k * H, 128), H)] = (sig[k] * inv).astype(BF16)
        return carry

    lax.fori_loop(0, 16, third_pass, 0)
    for axis in range(3):
        for d in range(1, 4):
            if axis:
                spread(axis, d).start()
        for d in range(1, 4):
            spread(axis, d).wait_recv()

    for d in range(8):
        swap(d).wait_send()
        if d:
            exchange(d).wait_send()
    for k in range(8):
        for kind, parts, to in FORWARD[k]:
            for part in parts:
                forward(k, kind, part, to).wait_send()

    def drain(s, carry):
        hand(s).wait_send()
        for side in range(2):
            first_hop(s, side).wait_send()
            second_hop(s, side).wait_send()
        beside(s).wait_send()
        return carry

    lax.fori_loop(0, 8, drain, 0)
    home_sibling().wait_send()

    def drain_home(s, carry):
        home(s, 0).wait_send()
        home(s, 1).wait_send()
        return carry

    lax.fori_loop(1, 8, drain_home, 0)
    pair(0).wait_send()
    pair(1).wait_send()
    for axis in range(3):
        for d in range(1, 4):
            spread(axis, d).wait_send()


def on_device(
    r_vector, r_previous, cycle_block, ladder_block, occ_energy, vir_energy, beta_previous
):
    row, col = lax.axis_index("row"), lax.axis_index("col")
    core = col % 2
    weights = jnp.transpose(ladder_block, (1, 0, 3, 2)).reshape(3 * O, 6 * O)
    dcol = (vir_energy[None, :] - occ_energy[:, None]).reshape(16, 1, H)
    occ_rows = lax.dynamic_slice(occ_energy, (core * HALF,), (HALF,))
    occ_rows = jnp.broadcast_to(occ_rows[:, None], (HALF, 128))
    mine = lax.dynamic_slice(beta_previous, (row * 8 + col // 2,), (1,))
    bprev = jnp.broadcast_to(mine[:, None], (8, 128))
    vmem, hbm = pl.BlockSpec(memory_space=pltpu.VMEM), pl.BlockSpec(memory_space=pl.ANY)
    dma = pltpu.SemaphoreType.DMA
    nxt, spread = pl.pallas_call(
        kernel,
        out_shape=(
            jax.ShapeDtypeStruct((HALF, O * V), BF16),
            jax.ShapeDtypeStruct((2, 4, 2, 4, 8, 128), F32),
        ),
        in_specs=[vmem, hbm, hbm, vmem, vmem, vmem, vmem],
        out_specs=(vmem, vmem),
        scratch_shapes=[
            pltpu.VMEM((2 * H, H), BF16),
            pltpu.VMEM((HALF, O * V), BF16),
            pltpu.VMEM((8, HALF, H), BF16),
            pltpu.VMEM((8, O, H), BF16),
            pltpu.VMEM((8, 2, 4, 2, O, H), BF16),
            pltpu.VMEM((8, 4, 2, O, H), F32),
            pltpu.VMEM((8, 2, O, H), F32),
            pltpu.VMEM((8, 2, 2, O, H), F32),
            pltpu.VMEM((8, O, H), F32),
            pltpu.VMEM((16, HALF, H), F32),
            pltpu.VMEM((2, 8, 128), F32),
            pltpu.VMEM((2, 8, 128), F32),
            dma((2,)), dma((8,)), dma((8,)), dma((8,)), dma((8,)),
            dma((len(SLOT),)), dma((8, 2)), dma((8,)), dma((8,)),
            dma((8, 2)), dma((8, 2)), dma((8, 2)), dma((8, 2)),
            dma((8,)), dma((8,)), dma((8, 2)), dma((16,)),
            dma((2,)), dma((2,)), dma((3, 3)), dma((3, 3)),
        ],
        compiler_params=pltpu.CompilerParams(
            collective_id=0, has_side_effects=True, vmem_limit_bytes=66 * 1024 * 1024 - 2 * 1024 * 1024 - 65536,
        ),
        name="sigma_step",
    )(r_vector, r_previous, cycle_block, weights, dcol, occ_rows, bprev)
    spread = spread.reshape(NVEC, 8, 128)
    return (nxt, spread[:, 0, 0], spread[:, 1, 0])


def solution(mesh):
    placed = (
        P(("row", "col"), None),
        P(("row", "col"), None),
        P("row", "col"),
        P(None, "col", None, "row"),
        P(),
        P(),
        P(),
    )
    return jax.shard_map(
        on_device,
        mesh=mesh,
        in_specs=placed,
        out_specs=(P(("row", "col"), None), P(), P()),
        check_vma=False,
    )
```

```python
import functools

import jax
import jax.numpy as jnp
from jax import lax
from jax.experimental import pallas as pl
from jax.experimental.pallas import tpu as pltpu
from jax.sharding import PartitionSpec as P

O = 48
V = 384
NVEC = 64
COUNT = O * O * V
H = 1152
HALF = O // 2
MESH = pl.DeviceIdType.MESH
ORDER = ((0, 0), (0, 1), (0, 3), (1, 0), (0, 2), (1, 1), (1, 3), (1, 2))
FORWARD = {
    0: (("down", (0, 1), 1), ("up", (0, 1), 2), ("across", (0, 1), 3)),
    1: (("down", (0,), 4),),
    2: (("up", (1,), 4),),
    3: (("down", (0, 1), 5), ("up", (0, 1), 6)),
    4: (),
    5: (("down", (0,), 7),),
    6: (("up", (1,), 7),),
    7: (),
}
SLOT = {}
for _t in range(8):
    for _kind, _parts, _to in FORWARD[_t]:
        for _p in _parts:
            SLOT[(_t, _kind, _p)] = len(SLOT)
F32 = jnp.float32
BF16 = jnp.bfloat16
TILES = 37
LEVELS = 32600.0
BIG = 12582912.0


def nearest(x):
    return (x + BIG) - BIG


def encode(src, dst):
    top = jnp.abs(src[:, 0:128])
    for k in range(1, H // 128):
        top = jnp.maximum(top, jnp.abs(src[:, k * 128:(k + 1) * 128]))
    peak = jnp.maximum(jnp.max(top), 1e-30)
    unit = jnp.full((8, 128), peak, F32) * (1.0 / LEVELS)
    dst[TILES - 1] = unit
    scale = 1.0 / unit
    for i in range(O // 8):
        rows = slice(i * 8, i * 8 + 8)
        for k in range(3):
            q = [nearest(src[rows, j * V + k * 128:j * V + k * 128 + 128] * scale) for j in range(3)]
            high = nearest(q[2] * (1.0 / 256.0))
            low = q[2] - high * 256.0
            dst[i * 3 + k] = q[0] * 512.0 + high
            dst[18 + i * 3 + k] = q[1] * 512.0 + low


def decode_add(msgs, dst):
    units = [m[TILES - 1] for m in msgs]
    for i in range(O // 8):
        rows = slice(i * 8, i * 8 + 8)
        for k in range(3):
            at = [slice(j * V + k * 128, j * V + k * 128 + 128) for j in range(3)]
            total = [dst[rows, a] for a in at]
            for m, unit in zip(msgs, units):
                one, two = m[i * 3 + k], m[18 + i * 3 + k]
                qa = nearest(one * (1.0 / 512.0))
                qb = nearest(two * (1.0 / 512.0))
                qc = (one - qa * 512.0) * 256.0 + (two - qb * 512.0)
                total = [t + v * unit for t, v in zip(total, (qa, qb, qc))]
            for a, t in zip(at, total):
                dst[rows, a] = t


def kernel(
    r_ref, prev_hbm, c_hbm, w_ref, vir_ref, occ_ref, bprev_ref,
    nxt_ref, g_ref,
    c_v, prev_v, sib, r48, ob, p, ao, ra, bo, tin, xo, xin, sig, st_out, st_in,
    load_sem, sib_s, sib_r, pa_s, pa_r, ag_s, ag_r, hs_s, hs_r,
    a_s, a_r, b_s, b_r, x_s, x_r, f_s, f_r, st_s, st_r, g_s, g_r,
):
    row, col = lax.axis_index("row"), lax.axis_index("col")
    xl, y = row // 4, row % 4
    xh, z, core = col // 8, (col % 8) // 2, col % 2

    def dev(xl_=None, y_=None, xh_=None, z_=None, core_=None):
        a = xl if xl_ is None else xl_
        b = y if y_ is None else y_
        c = xh if xh_ is None else xh_
        d = z if z_ is None else z_
        e = core if core_ is None else core_
        return (a * 4 + b, c * 8 + d * 2 + e)

    def remote(src, dst, ssem, rsem, to):
        return pltpu.make_async_remote_copy(
            src_ref=src, dst_ref=dst, send_sem=ssem, recv_sem=rsem,
            device_id=to, device_id_type=MESH,
        )

    y1, y2, y3 = (y + 1) % 4, (y + 2) % 4, (y + 3) % 4
    up, down = dev(z_=(z + 1) % 4), dev(z_=(z + 3) % 4)
    across = dev(xh_=1 - xh)
    sibling = dev(core_=1 - core)
    target = {"up": up, "down": down, "across": across}

    load_c = pltpu.make_async_copy(c_hbm, c_v, load_sem.at[0])
    load_p = pltpu.make_async_copy(prev_hbm, prev_v, load_sem.at[1])
    load_c.start()
    load_p.start()

    barrier = pltpu.get_barrier_semaphore()
    for d in range(1, 8):
        pl.semaphore_signal(barrier, inc=1, device_id=((row + d) % 8, col), device_id_type=MESH)
    for d in range(1, 16):
        pl.semaphore_signal(barrier, inc=1, device_id=(row, (col + d) % 16), device_id_type=MESH)
    pl.semaphore_signal(barrier, inc=1, device_id=dev(xl_=1 - xl, xh_=1 - xh), device_id_type=MESH)
    pl.semaphore_wait(barrier, 23)

    def rel(d):
        yd, xd = (y + d % 4) % 4, (xl + d // 4) % 2
        return yd, xd

    def cols(yd, xd, half):
        return pl.ds(pl.multiple_of(((xd * 4 + yd) * 2 + half) * H, 128), H)

    rel_order = (6, 2, 5, 7, 1, 3, 4, 0)

    def swap(d):
        yd, xd = rel(d)
        return remote(r_ref.at[:, cols(yd, xd, 1 - core)], sib.at[d], sib_s.at[d], sib_r.at[d], sibling)

    blk0 = xh * 4 + z

    def exchange(d):
        yd, xd = rel(d)
        return remote(r48.at[d], ob.at[blk0, core, y, xl], pa_s.at[d], pa_r.at[d], dev(xl_=xd, y_=yd))

    for d in rel_order:
        swap(d).start()
    for d in rel_order:
        yd, xd = rel(d)
        swap(d).wait_recv()
        mine = r_ref[:, cols(yd, xd, core)].astype(F32)
        other = sib[d].astype(F32)
        first = jnp.where(core == 0, mine, other)
        second = jnp.where(core == 0, other, mine)
        both = jnp.concatenate([first, second], axis=0).astype(BF16)
        if d == 0:
            ob[blk0, core, y, xl] = both
        else:
            r48[d] = both
            exchange(d).start()

    def block_of(t):
        out_x, out_z = xh, z
        for k, (dx, dz) in enumerate(ORDER):
            out_x = jnp.where(t == k, (xh + dx) % 2, out_x)
            out_z = jnp.where(t == k, (z + dz) % 4, out_z)
        return out_x, out_z

    def forward(t, kind, part, to):
        dx, dz = ORDER[t]
        blk = ((xh + dx) % 2) * 4 + (z + dz) % 4
        piece = ob.at[blk, core, pl.ds(2 * part, 2)]
        return remote(piece, piece, ag_s.at[SLOT[(t, kind, part)]], ag_r.at[to, part], target[kind])

    def hand(t):
        bx, bz = block_of(t)
        piece = ob.at[bx * 4 + bz, core]
        return remote(piece, piece, hs_s.at[t], hs_r.at[t], sibling)

    def landed(t, part):
        bx, bz = block_of(t)
        piece = ob.at[bx * 4 + bz, core, pl.ds(2 * part, 2)]
        return remote(piece, piece, ag_s.at[0], ag_r.at[t, part], sibling)

    def sibling_landed(t):
        bx, bz = block_of(t)
        piece = ob.at[bx * 4 + bz, 1 - core]
        return remote(piece, piece, hs_s.at[t], hs_r.at[t], sibling)

    def first_hop(s, side):
        to = dev(y_=y1) if side == 0 else dev(y_=y3)
        return remote(ao.at[s, side], ra.at[s, side], a_s.at[s, side], a_r.at[s, side], to)

    def second_hop(s, side, which):
        yd = y1 if side == 0 else y3
        return remote(
            bo.at[s, side, which], tin.at[s, side, which],
            b_s.at[s, side, which], b_r.at[s, side, which], dev(y_=yd),
        )

    def beside(s):
        return remote(xo.at[s], xin.at[s], x_s.at[s], x_r.at[s], dev(xl_=1 - xl))

    def home(s, core_to):
        bx, bz = block_of(s)
        return remote(
            p.at[s, y, xl, pl.ds(core_to * HALF, HALF)], sig.at[col],
            f_s.at[s, core_to], f_r.at[col], dev(xh_=bx, z_=bz, core_=core_to),
        )

    def home_sibling():
        return remote(
            p.at[0, y, xl, pl.ds(pl.multiple_of((1 - core) * HALF, 8), HALF)], sig.at[col],
            f_s.at[0, 0], f_r.at[col], sibling,
        )

    load_c.wait()

    def relay(s):
        for side in range(2):
            first_hop(s, side).wait_recv()
            share = p.at[s, y1 if side == 0 else y3, side]
            decode_add([ra.at[s, side]], share)
            encode(share, bo.at[s, side, side])
            second_hop(s, side, side).start()

    def across_pair(s):
        for side in range(2):
            for which in range(2):
                second_hop(s, side, which).wait_recv()
        decode_add([tin.at[s, 0, 1 - xl], tin.at[s, 1, 1 - xl]], p.at[s, y, 1 - xl])
        encode(p.at[s, y, 1 - xl], xo.at[s])
        beside(s).start()
        decode_add([tin.at[s, 0, xl], tin.at[s, 1, xl]], p.at[s, y, xl])

    def deliver(s):
        beside(s).wait_recv()
        decode_add([xin.at[s]], p.at[s, y, xl])

        @pl.when(s == 0)
        def _():
            home_sibling().start()
            sig[col] = p[0, y, xl, pl.ds(pl.multiple_of(core * HALF, 8), HALF)]

        @pl.when(s > 0)
        def _():
            home(s, 0).start()
            home(s, 1).start()

    def step(t, carry):
        @pl.when(t == 1)
        def _():
            relay(t - 1)
            across_pair(t - 1)
            deliver(t - 1)

        @pl.when(t == 0)
        def _():
            for d in range(1, 8):
                exchange(d).wait_recv()

        @pl.when(jnp.logical_and(t > 0, t < 8))
        def _():
            landed(t, 0).wait_recv()
            landed(t, 1).wait_recv()

        for k in range(8):
            if FORWARD[k]:
                @pl.when(t == k)
                def _(k=k):
                    for kind, parts, to in FORWARD[k]:
                        for part in parts:
                            forward(k, kind, part, to).start()

        @pl.when(t < 8)
        def _():
            hand(t).start()
            sibling_landed(t).wait_recv()
            bx, bz = block_of(t)
            blk = bx * 4 + bz
            x0 = ob[blk, 0].reshape(8 * O, H)
            x1 = ob[blk, 1].reshape(8 * O, H)
            acc = jnp.dot(x0, c_v[:H], preferred_element_type=F32)
            acc = acc + jnp.dot(x1, c_v[H:], preferred_element_type=F32)
            p[t] = acc.reshape(4, 2, O, H)

            def ladder(v, carry2):
                vy, vx = v // 2, v % 2
                stack = jnp.concatenate(
                    [ob[blk, h, vy, vx, :, q * V:(q + 1) * V] for h in range(2) for q in range(3)],
                    axis=0,
                )
                part = jnp.dot(w_ref[...], stack, preferred_element_type=F32)
                for j in range(3):
                    p[t, vy, vx, :, j * V:(j + 1) * V] += part[j * O:(j + 1) * O]
                return carry2

            lax.fori_loop(0, 8, ladder, 0)
            for side in range(2):
                encode(p.at[t, y2, side], ao.at[t, side])
                first_hop(t, side).start()
            for side in range(2):
                encode(p.at[t, y1 if side == 0 else y3, 1 - side], bo.at[t, side, 1 - side])
                second_hop(t, side, 1 - side).start()

        @pl.when(jnp.logical_and(t >= 2, t <= 8))
        def _():
            relay(t - 1)

        @pl.when(jnp.logical_and(t >= 3, t <= 9))
        def _():
            across_pair(t - 2)

        @pl.when(t >= 4)
        def _():
            deliver(t - 3)

        return carry

    lax.fori_loop(0, 11, step, 0)
    load_p.wait()

    def sums(val):
        total = val[:, 0:128]
        for k in range(1, H // 128):
            total = total + val[:, k * 128:(k + 1) * 128]
        return total[0:8] + total[8:16] + total[16:24]

    line24 = lax.broadcasted_iota(jnp.int32, (HALF, 128), 0)
    occ_mat = jnp.zeros((HALF, 128), F32)
    for i in range(HALF):
        occ_mat = jnp.where(line24 == i, occ_ref[core * HALF + i], occ_mat)
    occ_col = occ_mat[:, 0:1]
    vir_row = vir_ref[...]

    def arrived(d):
        from_col = (col + d) % 16
        return remote(sig.at[from_col], sig.at[from_col], f_s.at[0, 0], f_r.at[from_col], sibling)

    def first_pass(d, carry):
        acc_s, acc_r = carry
        @pl.when(d > 0)
        def _():
            arrived(d).wait_recv()
        k = (col + d) % 16
        rv = r_ref[:, pl.ds(pl.multiple_of(k * H, 128), H)].astype(F32)
        levels = jnp.concatenate([vir_row - occ_ref[k * 3 + j] for j in range(3)], axis=1)
        val = sig[k] + (levels - occ_col) * rv
        sig[k] = val
        return acc_s + sums(rv * val), acc_r + sums(rv * rv)

    zero = jnp.zeros((8, 128), F32)
    acc_s, acc_r = lax.fori_loop(0, 16, first_pass, (zero, zero))
    line = lax.broadcasted_iota(jnp.int32, (8, 128), 0)

    def pair(k):
        return remote(st_out.at[k], st_in.at[k], st_s.at[k], st_r.at[k], sibling)

    st_out[0] = jnp.where(line == 0, jnp.sum(acc_s), jnp.sum(acc_r))
    pair(0).start()
    pair(0).wait_recv()
    both = st_out[0] + st_in[0]
    alpha = both[0:1] / COUNT / (both[1:2] / COUNT + 1e-06)
    alpha_1 = alpha[:, 0:1]
    bprev_1 = bprev_ref[row * 8 + xh * 4 + z]

    def second_pass(k, acc):
        at = pl.ds(pl.multiple_of(k * H, 128), H)
        val = sig[k] - alpha_1 * r_ref[:, at].astype(F32) - bprev_1 * prev_v[:, at].astype(F32)
        sig[k] = val
        return acc + sums(val * val)

    acc_n = lax.fori_loop(0, 16, second_pass, zero)
    st_out[1] = jnp.where(line == 0, jnp.sum(acc_n), 0.0)
    pair(1).start()
    pair(1).wait_recv()
    norm = (st_out[1] + st_in[1])[0:1]
    beta = jnp.sqrt(norm / COUNT + 1e-06)
    inv = (1.0 / beta)[:, 0:1]

    g_ref[xl, y, xh, z] = jnp.where(line == 0, alpha, beta)

    def spread(axis, d):
        if axis == 0:
            piece, to = g_ref.at[xl, y, xh, z], dev(z_=(z + d) % 4)
        elif axis == 1:
            piece, to = g_ref.at[xl, y, xh], dev(y_=(y + d) % 4)
        else:
            piece = g_ref.at[xl, :, xh]
            to = dev(xl_=(xl + d % 2) % 2, xh_=(xh + d // 2) % 2)
        return remote(piece, piece, g_s.at[axis, d - 1], g_r.at[axis, d - 1], to)

    for d in range(1, 4):
        spread(0, d).start()

    def third_pass(k, carry):
        nxt_ref[:, pl.ds(pl.multiple_of(k * H, 128), H)] = (sig[k] * inv).astype(BF16)
        return carry

    lax.fori_loop(0, 16, third_pass, 0)
    for axis in range(3):
        for d in range(1, 4):
            if axis:
                spread(axis, d).start()
        for d in range(1, 4):
            spread(axis, d).wait_recv()

    for d in range(8):
        swap(d).wait_send()
        if d:
            exchange(d).wait_send()
    for k in range(8):
        for kind, parts, to in FORWARD[k]:
            for part in parts:
                forward(k, kind, part, to).wait_send()

    def drain(s, carry):
        hand(s).wait_send()
        for side in range(2):
            first_hop(s, side).wait_send()
            second_hop(s, side, 0).wait_send()
            second_hop(s, side, 1).wait_send()
        beside(s).wait_send()
        return carry

    lax.fori_loop(0, 8, drain, 0)
    home_sibling().wait_send()

    def drain_home(s, carry):
        home(s, 0).wait_send()
        home(s, 1).wait_send()
        return carry

    lax.fori_loop(1, 8, drain_home, 0)
    pair(0).wait_send()
    pair(1).wait_send()
    for axis in range(3):
        for d in range(1, 4):
            spread(axis, d).wait_send()


def on_device(
    r_vector, r_previous, cycle_block, ladder_block, occ_energy, vir_energy, beta_previous
):
    weights = jnp.transpose(ladder_block, (1, 0, 3, 2)).reshape(3 * O, 6 * O)
    vmem, hbm = pl.BlockSpec(memory_space=pltpu.VMEM), pl.BlockSpec(memory_space=pl.ANY)
    smem = pl.BlockSpec(memory_space=pltpu.SMEM)
    dma = pltpu.SemaphoreType.DMA
    nxt, spread = pl.pallas_call(
        kernel,
        out_shape=(
            jax.ShapeDtypeStruct((HALF, O * V), BF16),
            jax.ShapeDtypeStruct((2, 4, 2, 4, 8, 128), F32),
        ),
        in_specs=[vmem, hbm, hbm, vmem, vmem, smem, smem],
        out_specs=(vmem, vmem),
        scratch_shapes=[
            pltpu.VMEM((2 * H, H), BF16),
            pltpu.VMEM((HALF, O * V), BF16),
            pltpu.VMEM((8, HALF, H), BF16),
            pltpu.VMEM((8, O, H), BF16),
            pltpu.VMEM((8, 2, 4, 2, O, H), BF16),
            pltpu.VMEM((8, 4, 2, O, H), F32),
            pltpu.VMEM((8, 2, TILES, 8, 128), F32),
            pltpu.VMEM((8, 2, TILES, 8, 128), F32),
            pltpu.VMEM((8, 2, 2, TILES, 8, 128), F32),
            pltpu.VMEM((8, 2, 2, TILES, 8, 128), F32),
            pltpu.VMEM((8, TILES, 8, 128), F32),
            pltpu.VMEM((8, TILES, 8, 128), F32),
            pltpu.VMEM((16, HALF, H), F32),
            pltpu.VMEM((2, 8, 128), F32),
            pltpu.VMEM((2, 8, 128), F32),
            dma((2,)), dma((8,)), dma((8,)), dma((8,)), dma((8,)),
            dma((len(SLOT),)), dma((8, 2)), dma((8,)), dma((8,)),
            dma((8, 2)), dma((8, 2)), dma((8, 2, 2)), dma((8, 2, 2)),
            dma((8,)), dma((8,)), dma((8, 2)), dma((16,)),
            dma((2,)), dma((2,)), dma((3, 3)), dma((3, 3)),
        ],
        compiler_params=pltpu.CompilerParams(
            collective_id=0, has_side_effects=True, vmem_limit_bytes=66 * 1024 * 1024 - 2 * 1024 * 1024 - 65536,
        ),
        name="sigma_step",
    )(r_vector, r_previous, cycle_block, weights, vir_energy.reshape(1, V), occ_energy, beta_previous)
    spread = spread.reshape(NVEC, 8, 128)
    return (nxt, spread[:, 0, 0], spread[:, 1, 0])


def solution(mesh):
    placed = (
        P(("row", "col"), None),
        P(("row", "col"), None),
        P("row", "col"),
        P(None, "col", None, "row"),
        P(),
        P(),
        P(),
    )
    return jax.shard_map(
        on_device,
        mesh=mesh,
        in_specs=placed,
        out_specs=(P(("row", "col"), None), P(), P()),
        check_vma=False,
    )
```

```python
import functools

import jax
import jax.numpy as jnp
from jax import lax
from jax.experimental import pallas as pl
from jax.experimental.pallas import tpu as pltpu
from jax.sharding import PartitionSpec as P

O = 48
V = 384
NVEC = 64
COUNT = O * O * V
H = 1152
HALF = O // 2
MESH = pl.DeviceIdType.MESH
ORDER = ((0, 0), (0, 1), (0, 3), (1, 0), (0, 2), (1, 1), (1, 3), (1, 2))
FORWARD = {
    1: (("down", (0,), 4),),
    2: (("up", (1,), 4),),
    3: (("down", (0, 1), 5), ("up", (0, 1), 6)),
    5: (("down", (0,), 7),),
    6: (("up", (1,), 7),),
}
SLOT = {}
for _t in FORWARD:
    for _kind, _parts, _to in FORWARD[_t]:
        for _p in _parts:
            SLOT[(_t, _kind, _p)] = len(SLOT)
FIRST = (("down", 1), ("up", 2), ("across", 3))
F32 = jnp.float32
BF16 = jnp.bfloat16
HALVES = (
    (0, 0), (0, 1), (1, 0), (3, 0), (3, 1), (2, 0), (1, 1), (6, 0),
    (6, 1), (2, 1), (5, 0), (5, 1), (7, 0), (7, 1), (4, 0), (4, 1),
)
ARRIVALS = (
    (), (), ((3, 0), (1, 0),), (), ((3, 1), (2, 1), (2, 0),), ((1, 1),), (), ((5, 0), (6, 0),),
    ((6, 1),), (), ((5, 1),), ((4, 0),), ((7, 1), (7, 0),), ((4, 1),), (), (),
)
ROWS = HALF // 8
TILES = 6 * ROWS + 1
LEVELS = 43000.0
SPAN = 384.0
BIG = 12582912.0


def nearest(x):
    return (x + BIG) - BIG


def encode(src, dst):
    top = jnp.abs(src[:, 0:128])
    for k in range(1, H // 128):
        top = jnp.maximum(top, jnp.abs(src[:, k * 128:(k + 1) * 128]))
    peak = jnp.maximum(jnp.max(top), 1e-30)
    unit = jnp.full((8, 128), peak, F32) * (1.0 / LEVELS)
    dst[TILES - 1] = unit
    scale = 1.0 / unit
    for i in range(ROWS):
        rows = slice(i * 8, i * 8 + 8)
        for k in range(3):
            q = [nearest(src[rows, j * V + k * 128:j * V + k * 128 + 128] * scale) for j in range(3)]
            high = nearest(q[2] * (1.0 / 256.0))
            low = q[2] - high * 256.0
            dst[i * 3 + k] = q[0] * SPAN + high
            dst[3 * ROWS + i * 3 + k] = q[1] * SPAN + low


def decode_add(msgs, dst):
    units = [m[TILES - 1] for m in msgs]
    for i in range(ROWS):
        rows = slice(i * 8, i * 8 + 8)
        for k in range(3):
            at = [slice(j * V + k * 128, j * V + k * 128 + 128) for j in range(3)]
            total = [dst[rows, a] for a in at]
            for m, unit in zip(msgs, units):
                one, two = m[i * 3 + k], m[3 * ROWS + i * 3 + k]
                qa = nearest(one * (1.0 / SPAN))
                qb = nearest(two * (1.0 / SPAN))
                qc = (one - qa * SPAN) * 256.0 + (two - qb * SPAN)
                total = [t + v * unit for t, v in zip(total, (qa, qb, qc))]
            for a, t in zip(at, total):
                dst[rows, a] = t


def kernel(
    r_hbm, prev_hbm, c_hbm, w_hbm, vir_ref, occ_ref, bprev_ref,
    nxt_ref, g_ref,
    r_ref, w_ref, c_v, prev_v, sib, r48, ob, p, ao, ra, bo, tin, xo, xin, sig, st_out, st_in, g_out, g_in,
    load_sem, sib_s, sib_r, pa_s, pa_r, v_s, ag_s, ag_r, hs_s, hs_r,
    a_s, a_r, b_s, b_r, x_s, x_r, f_s, f_r, st_s, st_r, g_s, g_r,
):
    row, col = lax.axis_index("row"), lax.axis_index("col")
    xl, y = row // 4, row % 4
    xh, z, core = col // 8, (col % 8) // 2, col % 2

    def dev(xl_=None, y_=None, xh_=None, z_=None, core_=None):
        a = xl if xl_ is None else xl_
        b = y if y_ is None else y_
        c = xh if xh_ is None else xh_
        d = z if z_ is None else z_
        e = core if core_ is None else core_
        return (a * 4 + b, c * 8 + d * 2 + e)

    def remote(src, dst, ssem, rsem, to):
        return pltpu.make_async_remote_copy(
            src_ref=src, dst_ref=dst, send_sem=ssem, recv_sem=rsem,
            device_id=to, device_id_type=MESH,
        )

    y1, y2, y3 = (y + 1) % 4, (y + 2) % 4, (y + 3) % 4
    up, down = dev(z_=(z + 1) % 4), dev(z_=(z + 3) % 4)
    across = dev(xh_=1 - xh)
    sibling = dev(core_=1 - core)
    target = {"up": up, "down": down, "across": across}

    barrier = pltpu.get_barrier_semaphore()
    for d in range(1, 8):
        pl.semaphore_signal(barrier, inc=1, device_id=((row + d) % 8, col), device_id_type=MESH)
    for d in range(1, 16):
        pl.semaphore_signal(barrier, inc=1, device_id=(row, (col + d) % 16), device_id_type=MESH)
    pl.semaphore_signal(barrier, inc=1, device_id=dev(xl_=1 - xl, xh_=1 - xh), device_id_type=MESH)
    load_r = pltpu.make_async_copy(r_hbm, r_ref, load_sem.at[2])
    load_w = pltpu.make_async_copy(w_hbm, w_ref, load_sem.at[3])
    load_r.start()
    load_c = pltpu.make_async_copy(c_hbm, c_v, load_sem.at[0])
    load_p = pltpu.make_async_copy(prev_hbm, prev_v, load_sem.at[1])
    load_c.start()
    load_p.start()
    load_w.start()
    load_r.wait()
    pl.semaphore_wait(barrier, 23)

    def rel(d):
        yd, xd = (y + d % 4) % 4, (xl + d // 4) % 2
        return yd, xd

    def cols(yd, xd, half):
        return pl.ds(pl.multiple_of(((xd * 4 + yd) * 2 + half) * H, 128), H)

    near, far = (1, 3, 2), (4, 5, 7, 6)

    def swap(d):
        yd, xd = rel(d)
        return remote(r_ref.at[:, cols(yd, xd, 1 - core)], sib.at[d], sib_s.at[d], sib_r.at[d], sibling)

    blk0 = xh * 4 + z

    def exchange(d):
        yd, xd = rel(d)
        return remote(r48.at[d], ob.at[blk0, core, xl, y], pa_s.at[d], pa_r.at[d], dev(xl_=xd, y_=yd))

    def pass_on(d, to):
        kind, block = FIRST[to]
        ys, xs = (y + 4 - d % 4) % 4, (xl + d // 4) % 2
        piece = ob.at[blk0, core, xs, ys]
        return remote(piece, piece, v_s.at[to, d], ag_r.at[block, d // 4], target[kind])

    for d in (0,) + near + far:
        swap(d).start()
    for d in (0,) + near + far:
        yd, xd = rel(d)
        swap(d).wait_recv()
        mine = r_ref[:, cols(yd, xd, core)].astype(F32)
        other = sib[d].astype(F32)
        first = jnp.where(core == 0, mine, other)
        second = jnp.where(core == 0, other, mine)
        both = jnp.concatenate([first, second], axis=0).astype(BF16)
        if d == 0:
            ob[blk0, core, xl, y] = both
        else:
            r48[d] = both
            exchange(d).start()
    for to in range(3):
        pass_on(0, to).start()
    for d in near:
        exchange(d).wait_recv()
        for to in range(3):
            pass_on(d, to).start()

    def block_of(t):
        out_x, out_z = xh, z
        for k, (dx, dz) in enumerate(ORDER):
            out_x = jnp.where(t == k, (xh + dx) % 2, out_x)
            out_z = jnp.where(t == k, (z + dz) % 4, out_z)
        return out_x, out_z

    def forward(t, kind, part, to):
        dx, dz = ORDER[t]
        blk = ((xh + dx) % 2) * 4 + (z + dz) % 4
        piece = ob.at[blk, core, (part + xl) % 2]
        return remote(piece, piece, ag_s.at[SLOT[(t, kind, part)]], ag_r.at[to, part], target[kind])

    def hand(t, part):
        bx, bz = block_of(t)
        piece = ob.at[bx * 4 + bz, core, (part + xl) % 2]
        return remote(piece, piece, hs_s.at[t, part], hs_r.at[t, part], sibling)

    def landed(t, part):
        bx, bz = block_of(t)
        piece = ob.at[bx * 4 + bz, core, (part + xl) % 2]
        return remote(piece, piece, ag_s.at[0], ag_r.at[t, part], sibling)

    def sibling_landed(t, part):
        bx, bz = block_of(t)
        piece = ob.at[bx * 4 + bz, 1 - core, (part + xl) % 2]
        return remote(piece, piece, hs_s.at[t, part], hs_r.at[t, part], sibling)

    def half_of(u):
        t, g, keep = jnp.int32(0), jnp.int32(0), jnp.int32(0)
        for k, (bt, bg) in enumerate(HALVES):
            t, g = jnp.where(u == k, bt, t), jnp.where(u == k, bg, g)
            keep = jnp.where(u == k, HALVES.index((bt, 0)), keep)
        return t, g, keep

    def first_hop(s, side):
        to = dev(y_=y1) if side == 0 else dev(y_=y3)
        return remote(ao.at[s, side], ra.at[s, side], a_s.at[s, side], a_r.at[s, side], to)

    def second_hop(s, side, which):
        yd = y1 if side == 0 else y3
        return remote(
            bo.at[s, side, which], tin.at[s, side, which],
            b_s.at[s, side, which], b_r.at[s, side, which], dev(y_=yd),
        )

    def beside(t):
        return remote(xo.at[t], xin.at[t], x_s.at[t], x_r.at[t], dev(xl_=1 - xl))

    def home(t, keep, core_to):
        bx, bz = block_of(t)
        return remote(
            p.at[keep, y, pl.ds(core_to * HALF, HALF)], sig.at[col],
            f_s.at[t, core_to], f_r.at[col], dev(xh_=bx, z_=bz, core_=core_to),
        )

    def home_sibling():
        return remote(
            p.at[0, y, pl.ds(pl.multiple_of((1 - core) * HALF, 8), HALF)], sig.at[col],
            f_s.at[0, 0], f_r.at[col], sibling,
        )

    load_c.wait()
    load_w.wait()

    rows_of = (slice(0, HALF), slice(HALF, O))

    def relay(u):
        for side in range(2):
            first_hop(u, side).wait_recv()
            share = p.at[u, y1 if side == 0 else y3, rows_of[side]]
            decode_add([ra.at[u, side]], share)
            encode(share, bo.at[u, side, side])
            second_hop(u, side, side).start()

    def across_pair(u):
        t, g, _ = half_of(u)
        for which in range(2):
            second_hop(u, 0, which).wait_recv()
            second_hop(u, 1, which).wait_recv()
            decode_add([tin.at[u, 0, which], tin.at[u, 1, which]], p.at[u, y, rows_of[which]])

        @pl.when(g == 1)
        def _():
            for which in range(2):
                encode(p.at[u, y, rows_of[which]], xo.at[t, which])
            beside(t).start()

    def deliver(u):
        t, g, keep = half_of(u)

        @pl.when(g == 1)
        def _():
            beside(t).wait_recv()
            for which in range(2):
                decode_add([xin.at[t, which]], p.at[keep, y, rows_of[which]])

            @pl.when(t == 0)
            def _():
                home_sibling().start()
                sig[col] = p[0, y, pl.ds(pl.multiple_of(core * HALF, 8), HALF)]

            @pl.when(t > 0)
            def _():
                home(t, keep, 0).start()
                home(t, keep, 1).start()

    def step(u, carry):
        t, g, _ = half_of(u)

        @pl.when(u == 1)
        def _():
            for d in far:
                exchange(d).wait_recv()
                for to in range(3):
                    pass_on(d, to).start()

        @pl.when(u < 2)
        def _():
            hand(0, u).start()

        for k, todo in enumerate(ARRIVALS):
            if todo:
                @pl.when(u == k)
                def _(todo=todo):
                    for bt, part in todo:
                        landed(bt, part).wait_recv()
                        for kind, parts, to in FORWARD.get(bt, ()):
                            if part in parts:
                                forward(bt, kind, part, to).start()
                        hand(bt, part).start()

        @pl.when(u < 16)
        def _():
            sibling_landed(t, g).wait_recv()
            bx, bz = block_of(t)
            h = (g + xl) % 2
            blk = bx * 4 + bz
            x0 = ob[blk, 0, h].reshape(4 * O, H)
            x1 = ob[blk, 1, h].reshape(4 * O, H)
            acc = jnp.dot(x0, c_v[:H], preferred_element_type=F32)
            acc = acc + jnp.dot(x1, c_v[H:], preferred_element_type=F32)
            p[u] = acc.reshape(4, O, H)

            def ladder(v, carry2):
                stack = jnp.concatenate(
                    [ob[blk, w, h, v, :, q * V:(q + 1) * V] for w in range(2) for q in range(3)],
                    axis=0,
                )
                part = jnp.dot(w_ref[...], stack, preferred_element_type=F32)
                for j in range(3):
                    p[u, v, :, j * V:(j + 1) * V] += part[j * O:(j + 1) * O]
                return carry2

            lax.fori_loop(0, 4, ladder, 0)
            for side in range(2):
                encode(p.at[u, y2, rows_of[side]], ao.at[u, side])
                first_hop(u, side).start()
            for side in range(2):
                encode(p.at[u, y1 if side == 0 else y3, rows_of[1 - side]], bo.at[u, side, 1 - side])
                second_hop(u, side, 1 - side).start()

        @pl.when(jnp.logical_and(u >= 1, u <= 16))
        def _():
            relay(u - 1)

        @pl.when(jnp.logical_and(u >= 2, u <= 17))
        def _():
            across_pair(u - 2)

        @pl.when(u >= 3)
        def _():
            deliver(u - 3)

        return carry

    lax.fori_loop(0, 19, step, 0)
    load_p.wait()

    def sums(val):
        total = val[:, 0:128]
        for k in range(1, H // 128):
            total = total + val[:, k * 128:(k + 1) * 128]
        return total[0:8] + total[8:16] + total[16:24]

    line24 = lax.broadcasted_iota(jnp.int32, (HALF, 128), 0)
    occ_mat = jnp.zeros((HALF, 128), F32)
    for i in range(HALF):
        occ_mat = jnp.where(line24 == i, occ_ref[core * HALF + i], occ_mat)
    occ_col = occ_mat[:, 0:1]
    vir_row = vir_ref[...].reshape(1, V)

    def arrived(d):
        from_col = (col + d) % 16
        return remote(sig.at[from_col], sig.at[from_col], f_s.at[0, 0], f_r.at[from_col], sibling)

    def first_pass(d, carry):
        acc_s, acc_r = carry
        @pl.when(d > 0)
        def _():
            arrived(d).wait_recv()
        k = (col + d) % 16
        rv = r_ref[:, pl.ds(pl.multiple_of(k * H, 128), H)].astype(F32)
        levels = jnp.concatenate([vir_row - occ_ref[k * 3 + j] for j in range(3)], axis=1)
        val = sig[k] + (levels - occ_col) * rv
        sig[k] = val
        return acc_s + sums(rv * val), acc_r + sums(rv * rv)

    zero = jnp.zeros((8, 128), F32)
    acc_s, acc_r = lax.fori_loop(0, 16, first_pass, (zero, zero))
    line = lax.broadcasted_iota(jnp.int32, (8, 128), 0)

    def pair(k):
        return remote(st_out.at[k], st_in.at[k], st_s.at[k], st_r.at[k], sibling)

    st_out[0] = jnp.where(line == 0, jnp.sum(acc_s), jnp.sum(acc_r))
    pair(0).start()
    pair(0).wait_recv()
    both = st_out[0] + st_in[0]
    alpha = both[0:1] / COUNT / (both[1:2] / COUNT + 1e-06)
    alpha_1 = alpha[:, 0:1]
    bprev_1 = bprev_ref[row * 8 + xh * 4 + z]

    def second_pass(k, acc):
        at = pl.ds(pl.multiple_of(k * H, 128), H)
        val = sig[k] - alpha_1 * r_ref[:, at].astype(F32) - bprev_1 * prev_v[:, at].astype(F32)
        sig[k] = val
        return acc + sums(val * val)

    acc_n = lax.fori_loop(0, 16, second_pass, zero)
    st_out[1] = jnp.where(line == 0, jnp.sum(acc_n), 0.0)
    pair(1).start()
    pair(1).wait_recv()
    norm = (st_out[1] + st_in[1])[0:1]
    beta = jnp.sqrt(norm / COUNT + 1e-06)
    inv = (1.0 / beta)[:, 0:1]

    lane = lax.broadcasted_iota(jnp.int32, (8, 128), 1)
    vec = row * 8 + xh * 4 + z
    g_out[0] = jnp.where(lane == vec, jnp.where(line == 0, alpha, beta), 0.0)

    def spread(axis, d):
        if axis == 0:
            to = dev(z_=(z + d) % 4)
        elif axis == 1:
            to = dev(y_=(y + d) % 4)
        else:
            to = dev(xl_=(xl + d % 2) % 2, xh_=(xh + d // 2) % 2)
        return remote(g_out.at[axis], g_in.at[axis, d - 1], g_s.at[axis, d - 1], g_r.at[axis, d - 1], to)

    for d in range(1, 4):
        spread(0, d).start()

    def third_pass(k, carry):
        nxt_ref[:, pl.ds(pl.multiple_of(k * H, 128), H)] = (sig[k] * inv).astype(BF16)
        return carry

    lax.fori_loop(0, 16, third_pass, 0)
    for axis in range(3):
        for d in range(1, 4):
            spread(axis, d).wait_recv()
        merged = g_out[axis] + g_in[axis, 0] + g_in[axis, 1] + g_in[axis, 2]
        if axis == 2:
            g_ref[...] = merged
        else:
            g_out[axis + 1] = merged
            for d in range(1, 4):
                spread(axis + 1, d).start()

    for d in range(8):
        swap(d).wait_send()
        if d:
            exchange(d).wait_send()
        for to in range(3):
            pass_on(d, to).wait_send()
    for bt in FORWARD:
        for kind, parts, to in FORWARD[bt]:
            for part in parts:
                forward(bt, kind, part, to).wait_send()

    def drain(u, carry):
        t, g, keep = half_of(u)
        hand(t, g).wait_send()
        for side in range(2):
            first_hop(u, side).wait_send()
            second_hop(u, side, 0).wait_send()
            second_hop(u, side, 1).wait_send()

        @pl.when(g == 1)
        def _():
            beside(t).wait_send()

            @pl.when(t == 0)
            def _():
                home_sibling().wait_send()

            @pl.when(t > 0)
            def _():
                home(t, keep, 0).wait_send()
                home(t, keep, 1).wait_send()

        return carry

    lax.fori_loop(0, 16, drain, 0)
    pair(0).wait_send()
    pair(1).wait_send()
    for axis in range(3):
        for d in range(1, 4):
            spread(axis, d).wait_send()


def on_device(
    r_vector, r_previous, cycle_block, ladder_block, occ_energy, vir_energy, beta_previous
):
    weights = jnp.transpose(ladder_block, (1, 0, 3, 2)).reshape(3 * O, 6 * O)
    vmem, hbm = pl.BlockSpec(memory_space=pltpu.VMEM), pl.BlockSpec(memory_space=pl.ANY)
    smem = pl.BlockSpec(memory_space=pltpu.SMEM)
    dma = pltpu.SemaphoreType.DMA
    nxt, spread = pl.pallas_call(
        kernel,
        out_shape=(
            jax.ShapeDtypeStruct((HALF, O * V), BF16),
            jax.ShapeDtypeStruct((8, 128), F32),
        ),
        in_specs=[hbm, hbm, hbm, hbm, vmem, smem, smem],
        out_specs=(vmem, vmem),
        scratch_shapes=[
            pltpu.VMEM((HALF, O * V), BF16),
            pltpu.VMEM((3 * O, 6 * O), BF16),
            pltpu.VMEM((2 * H, H), BF16),
            pltpu.VMEM((HALF, O * V), BF16),
            pltpu.VMEM((8, HALF, H), BF16),
            pltpu.VMEM((8, O, H), BF16),
            pltpu.VMEM((8, 2, 2, 4, O, H), BF16),
            pltpu.VMEM((16, 4, O, H), F32),
            pltpu.VMEM((16, 2, TILES, 8, 128), F32),
            pltpu.VMEM((16, 2, TILES, 8, 128), F32),
            pltpu.VMEM((16, 2, 2, TILES, 8, 128), F32),
            pltpu.VMEM((16, 2, 2, TILES, 8, 128), F32),
            pltpu.VMEM((8, 2, TILES, 8, 128), F32),
            pltpu.VMEM((8, 2, TILES, 8, 128), F32),
            pltpu.VMEM((16, HALF, H), F32),
            pltpu.VMEM((2, 8, 128), F32),
            pltpu.VMEM((2, 8, 128), F32),
            pltpu.VMEM((3, 8, 128), F32),
            pltpu.VMEM((3, 3, 8, 128), F32),
            dma((4,)), dma((8,)), dma((8,)), dma((8,)), dma((8,)), dma((3, 8)),
            dma((len(SLOT),)), dma((8, 2)), dma((8, 2)), dma((8, 2)),
            dma((16, 2)), dma((16, 2)), dma((16, 2, 2)), dma((16, 2, 2)),
            dma((8,)), dma((8,)), dma((8, 2)), dma((16,)),
            dma((2,)), dma((2,)), dma((3, 3)), dma((3, 3)),
        ],
        compiler_params=pltpu.CompilerParams(
            collective_id=0, has_side_effects=True, vmem_limit_bytes=66 * 1024 * 1024 - 2 * 1024 * 1024 - 65536,
        ),
        name="sigma_step",
    )(r_vector, r_previous, cycle_block, weights, vir_energy, occ_energy, beta_previous)
    return (nxt, spread[0, :NVEC], spread[1, :NVEC])


def solution(mesh):
    placed = (
        P(("row", "col"), None),
        P(("row", "col"), None),
        P("row", "col"),
        P(None, "col", None, "row"),
        P(),
        P(),
        P(),
    )
    return jax.shard_map(
        on_device,
        mesh=mesh,
        in_specs=placed,
        out_specs=(P(("row", "col"), None), P(), P()),
        check_vma=False,
    )
```

```python
import functools

import jax
import jax.numpy as jnp
from jax import lax
from jax.experimental import pallas as pl
from jax.experimental.pallas import tpu as pltpu
from jax.sharding import PartitionSpec as P

O = 48
V = 384
NVEC = 64
COUNT = O * O * V
H = 1152
HALF = O // 2
MESH = pl.DeviceIdType.MESH
ORDER = ((0, 0), (0, 1), (0, 3), (1, 0), (0, 2), (1, 1), (1, 3), (1, 2))
FORWARD = {
    1: (("down", (0,), 4),),
    2: (("up", (1,), 4),),
    3: (("down", (0, 1), 5), ("up", (0, 1), 6)),
    5: (("down", (0,), 7),),
    6: (("up", (1,), 7),),
}
SLOT = {}
for _t in FORWARD:
    for _kind, _parts, _to in FORWARD[_t]:
        for _p in _parts:
            SLOT[(_t, _kind, _p)] = len(SLOT)
FIRST = (("down", 1), ("up", 2), ("across", 3))
F32 = jnp.float32
BF16 = jnp.bfloat16
HALVES = (
    (0, 0), (0, 1), (1, 0), (3, 0), (3, 1), (2, 0), (1, 1), (6, 0),
    (2, 1), (6, 1), (5, 0), (5, 1), (7, 0), (7, 1), (4, 0), (4, 1),
)
ARRIVALS = (
    (), (), ((3, 0), (1, 0),), (), ((2, 0), (1, 1), (3, 1), (2, 1),), (), ((6, 0), (5, 0),), (),
    ((4, 0),), ((6, 1),), ((5, 1),), (), ((7, 1), (4, 1), (7, 0),), (), (), (),
)
ROWS = HALF // 8
TILES = 6 * ROWS + 1
LEVELS = 43000.0
SPAN = 384.0
BIG = 12582912.0


def nearest(x):
    return (x + BIG) - BIG


def encode(src, dst):
    top = jnp.abs(src[:, 0:128])
    for k in range(1, H // 128):
        top = jnp.maximum(top, jnp.abs(src[:, k * 128:(k + 1) * 128]))
    peak = jnp.maximum(jnp.max(top), 1e-30)
    unit = jnp.full((8, 128), peak, F32) * (1.0 / LEVELS)
    dst[TILES - 1] = unit
    scale = 1.0 / unit
    for i in range(ROWS):
        rows = slice(i * 8, i * 8 + 8)
        for k in range(3):
            q = [nearest(src[rows, j * V + k * 128:j * V + k * 128 + 128] * scale) for j in range(3)]
            high = nearest(q[2] * (1.0 / 256.0))
            low = q[2] - high * 256.0
            dst[i * 3 + k] = q[0] * SPAN + high
            dst[3 * ROWS + i * 3 + k] = q[1] * SPAN + low


def decode_add(msgs, dst):
    units = [m[TILES - 1] for m in msgs]
    for i in range(ROWS):
        rows = slice(i * 8, i * 8 + 8)
        for k in range(3):
            at = [slice(j * V + k * 128, j * V + k * 128 + 128) for j in range(3)]
            total = [dst[rows, a] for a in at]
            for m, unit in zip(msgs, units):
                one, two = m[i * 3 + k], m[3 * ROWS + i * 3 + k]
                qa = nearest(one * (1.0 / SPAN))
                qb = nearest(two * (1.0 / SPAN))
                qc = (one - qa * SPAN) * 256.0 + (two - qb * SPAN)
                total = [t + v * unit for t, v in zip(total, (qa, qb, qc))]
            for a, t in zip(at, total):
                dst[rows, a] = t


def decode_set(msg, dst):
    unit = msg[TILES - 1]
    for i in range(ROWS):
        rows = slice(i * 8, i * 8 + 8)
        for k in range(3):
            one, two = msg[i * 3 + k], msg[3 * ROWS + i * 3 + k]
            qa = nearest(one * (1.0 / SPAN))
            qb = nearest(two * (1.0 / SPAN))
            qc = (one - qa * SPAN) * 256.0 + (two - qb * SPAN)
            for j, v in enumerate((qa, qb, qc)):
                dst[rows, j * V + k * 128:j * V + k * 128 + 128] = v * unit


def kernel(
    r_hbm, prev_hbm, c_hbm, w_hbm, vir_ref, occ_ref, bprev_ref,
    nxt_ref, g_ref,
    r_ref, w_ref, c_v, prev_v, sib, r48, ob, p, ao, ra, bo, tin, xo, xin, ho, hin, sig, st_out, st_in, g_out, g_in,
    load_sem, sib_s, sib_r, pa_s, pa_r, v_s, ag_s, ag_r, hs_s, hs_r,
    a_s, a_r, b_s, b_r, x_s, x_r, f_s, f_r, st_s, st_r, g_s, g_r,
):
    row, col = lax.axis_index("row"), lax.axis_index("col")
    xl, y = row // 4, row % 4
    xh, z, core = col // 8, (col % 8) // 2, col % 2

    def dev(xl_=None, y_=None, xh_=None, z_=None, core_=None):
        a = xl if xl_ is None else xl_
        b = y if y_ is None else y_
        c = xh if xh_ is None else xh_
        d = z if z_ is None else z_
        e = core if core_ is None else core_
        return (a * 4 + b, c * 8 + d * 2 + e)

    def remote(src, dst, ssem, rsem, to):
        return pltpu.make_async_remote_copy(
            src_ref=src, dst_ref=dst, send_sem=ssem, recv_sem=rsem,
            device_id=to, device_id_type=MESH,
        )

    y1, y2, y3 = (y + 1) % 4, (y + 2) % 4, (y + 3) % 4
    up, down = dev(z_=(z + 1) % 4), dev(z_=(z + 3) % 4)
    across = dev(xh_=1 - xh)
    sibling = dev(core_=1 - core)
    target = {"up": up, "down": down, "across": across}

    barrier = pltpu.get_barrier_semaphore()
    for d in range(1, 8):
        pl.semaphore_signal(barrier, inc=1, device_id=((row + d) % 8, col), device_id_type=MESH)
    for d in range(1, 16):
        pl.semaphore_signal(barrier, inc=1, device_id=(row, (col + d) % 16), device_id_type=MESH)
    pl.semaphore_signal(barrier, inc=1, device_id=dev(xl_=1 - xl, xh_=1 - xh), device_id_type=MESH)
    load_r = pltpu.make_async_copy(r_hbm, r_ref, load_sem.at[2])
    load_w = pltpu.make_async_copy(w_hbm, w_ref, load_sem.at[3])
    load_r.start()
    load_c = pltpu.make_async_copy(c_hbm, c_v, load_sem.at[0])
    load_p = pltpu.make_async_copy(prev_hbm, prev_v, load_sem.at[1])
    load_c.start()
    load_p.start()
    load_w.start()
    load_r.wait()
    pl.semaphore_wait(barrier, 23)

    def rel(d):
        yd, xd = (y + d % 4) % 4, (xl + d // 4) % 2
        return yd, xd

    def cols(yd, xd, half):
        return pl.ds(pl.multiple_of(((xd * 4 + yd) * 2 + half) * H, 128), H)

    near, far = (1, 3, 2), (4, 5, 7, 6)

    def swap(d):
        yd, xd = rel(d)
        return remote(r_ref.at[:, cols(yd, xd, 1 - core)], sib.at[d], sib_s.at[d], sib_r.at[d], sibling)

    blk0 = xh * 4 + z

    def exchange(d):
        yd, xd = rel(d)
        return remote(r48.at[d], ob.at[blk0, core, xl, y], pa_s.at[d], pa_r.at[d], dev(xl_=xd, y_=yd))

    def pass_on(d, to):
        kind, block = FIRST[to]
        ys, xs = (y + 4 - d % 4) % 4, (xl + d // 4) % 2
        piece = ob.at[blk0, core, xs, ys]
        return remote(piece, piece, v_s.at[to, d], ag_r.at[block, d // 4], target[kind])

    for d in (0,) + near + far:
        swap(d).start()
    def prepare(d):
        yd, xd = rel(d)
        swap(d).wait_recv()
        mine = r_ref[:, cols(yd, xd, core)].astype(F32)
        other = sib[d].astype(F32)
        first = jnp.where(core == 0, mine, other)
        second = jnp.where(core == 0, other, mine)
        both = jnp.concatenate([first, second], axis=0).astype(BF16)
        if d == 0:
            ob[blk0, core, xl, y] = both
        else:
            r48[d] = both
            exchange(d).start()

    for d in (0, 2, 1, 3, 6, 5, 7, 4):
        prepare(d)
    for to in range(3):
        pass_on(0, to).start()
    for d in near:
        exchange(d).wait_recv()
        for to in range(3):
            pass_on(d, to).start()

    def block_of(t):
        out_x, out_z = xh, z
        for k, (dx, dz) in enumerate(ORDER):
            out_x = jnp.where(t == k, (xh + dx) % 2, out_x)
            out_z = jnp.where(t == k, (z + dz) % 4, out_z)
        return out_x, out_z

    def forward(t, kind, part, to):
        dx, dz = ORDER[t]
        blk = ((xh + dx) % 2) * 4 + (z + dz) % 4
        piece = ob.at[blk, core, (part + xl) % 2]
        return remote(piece, piece, ag_s.at[SLOT[(t, kind, part)]], ag_r.at[to, part], target[kind])

    def hand(t, part):
        bx, bz = block_of(t)
        piece = ob.at[bx * 4 + bz, core, (part + xl) % 2]
        return remote(piece, piece, hs_s.at[t, part], hs_r.at[t, part], sibling)

    def landed(t, part):
        bx, bz = block_of(t)
        piece = ob.at[bx * 4 + bz, core, (part + xl) % 2]
        return remote(piece, piece, ag_s.at[0], ag_r.at[t, part], sibling)

    def sibling_landed(t, part):
        bx, bz = block_of(t)
        piece = ob.at[bx * 4 + bz, 1 - core, (part + xl) % 2]
        return remote(piece, piece, hs_s.at[t, part], hs_r.at[t, part], sibling)

    def half_of(u):
        t, g, keep = jnp.int32(0), jnp.int32(0), jnp.int32(0)
        for k, (bt, bg) in enumerate(HALVES):
            t, g = jnp.where(u == k, bt, t), jnp.where(u == k, bg, g)
            keep = jnp.where(u == k, HALVES.index((bt, 0)), keep)
        return t, g, keep

    def first_hop(s, side):
        to = dev(y_=y1) if side == 0 else dev(y_=y3)
        return remote(ao.at[s, side], ra.at[s, side], a_s.at[s, side], a_r.at[s, side], to)

    def second_hop(s, side, which):
        yd = y1 if side == 0 else y3
        return remote(
            bo.at[s, side, which], tin.at[s, side, which],
            b_s.at[s, side, which], b_r.at[s, side, which], dev(y_=yd),
        )

    def beside(t):
        return remote(xo.at[t], xin.at[t], x_s.at[t], x_r.at[t], dev(xl_=1 - xl))

    def home(t, core_to):
        bx, bz = block_of(t)
        return remote(
            ho.at[t, core_to], hin.at[col], f_s.at[t, core_to], f_r.at[col],
            dev(xh_=bx, z_=bz, core_=core_to),
        )

    def home_sibling():
        return remote(ho.at[0, 0], hin.at[col], f_s.at[0, 0], f_r.at[col], sibling)

    load_c.wait()
    load_w.wait()

    rows_of = (slice(0, HALF), slice(HALF, O))

    def relay(u):
        for side in range(2):
            first_hop(u, side).wait_recv()
            share = p.at[u, y1 if side == 0 else y3, rows_of[side]]
            decode_add([ra.at[u, side]], share)
            encode(share, bo.at[u, side, side])
            second_hop(u, side, side).start()

    def across_pair(u):
        t, g, _ = half_of(u)
        for which in range(2):
            second_hop(u, 0, which).wait_recv()
            second_hop(u, 1, which).wait_recv()
            decode_add([tin.at[u, 0, which], tin.at[u, 1, which]], p.at[u, y, rows_of[which]])

        @pl.when(g == 1)
        def _():
            for which in range(2):
                encode(p.at[u, y, rows_of[which]], xo.at[t, which])
            beside(t).start()

    def deliver(u):
        t, g, keep = half_of(u)

        @pl.when(g == 1)
        def _():
            beside(t).wait_recv()
            for which in range(2):
                decode_add([xin.at[t, which]], p.at[keep, y, rows_of[which]])

            @pl.when(t == 0)
            def _():
                encode(p.at[0, y, pl.ds(pl.multiple_of((1 - core) * HALF, 8), HALF)], ho.at[0, 0])
                home_sibling().start()
                sig[col] = p[0, y, pl.ds(pl.multiple_of(core * HALF, 8), HALF)]

            @pl.when(t > 0)
            def _():
                for which in range(2):
                    encode(p.at[keep, y, rows_of[which]], ho.at[t, which])
                    home(t, which).start()

    def step(u, carry):
        t, g, _ = half_of(u)

        @pl.when(u < 2)
        def _():
            hand(0, u).start()

        for k, todo in enumerate(ARRIVALS):
            if todo:
                @pl.when(u == k)
                def _(todo=todo):
                    for bt, part in todo:
                        landed(bt, part).wait_recv()
                        for kind, parts, to in FORWARD.get(bt, ()):
                            if part in parts:
                                forward(bt, kind, part, to).start()
                        hand(bt, part).start()

        @pl.when(u < 16)
        def _():
            sibling_landed(t, g).wait_recv()
            bx, bz = block_of(t)
            h = (g + xl) % 2
            blk = bx * 4 + bz
            x0 = ob[blk, 0, h].reshape(4 * O, H)
            x1 = ob[blk, 1, h].reshape(4 * O, H)
            acc = jnp.dot(x0, c_v[:H], preferred_element_type=F32)
            acc = acc + jnp.dot(x1, c_v[H:], preferred_element_type=F32)
            p[u] = acc.reshape(4, O, H)

            def ladder(v, carry2):
                stack = jnp.concatenate(
                    [ob[blk, w, h, v, :, q * V:(q + 1) * V] for w in range(2) for q in range(3)],
                    axis=0,
                )
                part = jnp.dot(w_ref[...], stack, preferred_element_type=F32)
                for j in range(3):
                    p[u, v, :, j * V:(j + 1) * V] += part[j * O:(j + 1) * O]
                return carry2

            @pl.when(u == 0)
            def _():
                for d in far:
                    exchange(d).wait_recv()
                    for to in range(3):
                        pass_on(d, to).start()

            ladder(y2, 0)
            for side in range(2):
                encode(p.at[u, y2, rows_of[side]], ao.at[u, side])
                first_hop(u, side).start()
            for side in range(2):
                yd = y1 if side == 0 else y3
                ladder(yd, 0)
                encode(p.at[u, yd, rows_of[1 - side]], bo.at[u, side, 1 - side])
                second_hop(u, side, 1 - side).start()
            ladder(y, 0)

        @pl.when(jnp.logical_and(u >= 1, u <= 16))
        def _():
            relay(u - 1)

        @pl.when(jnp.logical_and(u >= 3, u <= 18))
        def _():
            across_pair(u - 3)

        @pl.when(u >= 4)
        def _():
            deliver(u - 4)

        return carry

    lax.fori_loop(0, 20, step, 0)
    load_p.wait()

    def sums(val):
        total = val[:, 0:128]
        for k in range(1, H // 128):
            total = total + val[:, k * 128:(k + 1) * 128]
        return total[0:8] + total[8:16] + total[16:24]

    line24 = lax.broadcasted_iota(jnp.int32, (HALF, 128), 0)
    occ_mat = jnp.zeros((HALF, 128), F32)
    for i in range(HALF):
        occ_mat = jnp.where(line24 == i, occ_ref[core * HALF + i], occ_mat)
    occ_col = occ_mat[:, 0:1]
    vir_row = vir_ref[...].reshape(1, V)

    def arrived(d):
        from_col = (col + d) % 16
        return remote(ho.at[0, 0], hin.at[from_col], f_s.at[0, 0], f_r.at[from_col], sibling)

    def first_pass(d, carry):
        acc_s, acc_r = carry
        @pl.when(d > 0)
        def _():
            arrived(d).wait_recv()
            decode_set(hin.at[(col + d) % 16], sig.at[(col + d) % 16])
        k = (col + d) % 16
        rv = r_ref[:, pl.ds(pl.multiple_of(k * H, 128), H)].astype(F32)
        levels = jnp.concatenate([vir_row - occ_ref[k * 3 + j] for j in range(3)], axis=1)
        val = sig[k] + (levels - occ_col) * rv
        sig[k] = val
        return acc_s + sums(rv * val), acc_r + sums(rv * rv)

    zero = jnp.zeros((8, 128), F32)
    acc_s, acc_r = lax.fori_loop(0, 16, first_pass, (zero, zero))
    line = lax.broadcasted_iota(jnp.int32, (8, 128), 0)

    def pair(k):
        return remote(st_out.at[k], st_in.at[k], st_s.at[k], st_r.at[k], sibling)

    st_out[0] = jnp.where(line == 0, jnp.sum(acc_s), jnp.sum(acc_r))
    pair(0).start()
    pair(0).wait_recv()
    both = st_out[0] + st_in[0]
    alpha = both[0:1] / COUNT / (both[1:2] / COUNT + 1e-06)
    alpha_1 = alpha[:, 0:1]
    bprev_1 = bprev_ref[row * 8 + xh * 4 + z]

    def second_pass(k, acc):
        at = pl.ds(pl.multiple_of(k * H, 128), H)
        val = sig[k] - alpha_1 * r_ref[:, at].astype(F32) - bprev_1 * prev_v[:, at].astype(F32)
        sig[k] = val
        return acc + sums(val * val)

    acc_n = lax.fori_loop(0, 16, second_pass, zero)
    st_out[1] = jnp.where(line == 0, jnp.sum(acc_n), 0.0)
    pair(1).start()
    pair(1).wait_recv()
    norm = (st_out[1] + st_in[1])[0:1]
    beta = jnp.sqrt(norm / COUNT + 1e-06)
    inv = (1.0 / beta)[:, 0:1]

    lane = lax.broadcasted_iota(jnp.int32, (8, 128), 1)
    vec = row * 8 + xh * 4 + z
    g_out[0] = jnp.where(lane == vec, jnp.where(line == 0, alpha, beta), 0.0)

    def spread(axis, d):
        if axis == 0:
            to = dev(z_=(z + d) % 4)
        elif axis == 1:
            to = dev(y_=(y + d) % 4)
        else:
            to = dev(xl_=(xl + d % 2) % 2, xh_=(xh + d // 2) % 2)
        return remote(g_out.at[axis], g_in.at[axis, d - 1], g_s.at[axis, d - 1], g_r.at[axis, d - 1], to)

    for d in range(1, 4):
        spread(0, d).start()

    def third_pass(k, carry):
        nxt_ref[:, pl.ds(pl.multiple_of(k * H, 128), H)] = (sig[k] * inv).astype(BF16)
        return carry

    lax.fori_loop(0, 16, third_pass, 0)
    for axis in range(3):
        for d in range(1, 4):
            spread(axis, d).wait_recv()
        merged = g_out[axis] + g_in[axis, 0] + g_in[axis, 1] + g_in[axis, 2]
        if axis == 2:
            g_ref[...] = merged
        else:
            g_out[axis + 1] = merged
            for d in range(1, 4):
                spread(axis + 1, d).start()

    for d in range(8):
        swap(d).wait_send()
        if d:
            exchange(d).wait_send()
        for to in range(3):
            pass_on(d, to).wait_send()
    for bt in FORWARD:
        for kind, parts, to in FORWARD[bt]:
            for part in parts:
                forward(bt, kind, part, to).wait_send()

    def drain(u, carry):
        t, g, keep = half_of(u)
        hand(t, g).wait_send()
        for side in range(2):
            first_hop(u, side).wait_send()
            second_hop(u, side, 0).wait_send()
            second_hop(u, side, 1).wait_send()

        @pl.when(g == 1)
        def _():
            beside(t).wait_send()

            @pl.when(t == 0)
            def _():
                home_sibling().wait_send()

            @pl.when(t > 0)
            def _():
                home(t, 0).wait_send()
                home(t, 1).wait_send()

        return carry

    lax.fori_loop(0, 16, drain, 0)
    pair(0).wait_send()
    pair(1).wait_send()
    for axis in range(3):
        for d in range(1, 4):
            spread(axis, d).wait_send()


def on_device(
    r_vector, r_previous, cycle_block, ladder_block, occ_energy, vir_energy, beta_previous
):
    weights = jnp.transpose(ladder_block, (1, 0, 3, 2)).reshape(3 * O, 6 * O)
    vmem, hbm = pl.BlockSpec(memory_space=pltpu.VMEM), pl.BlockSpec(memory_space=pl.ANY)
    smem = pl.BlockSpec(memory_space=pltpu.SMEM)
    dma = pltpu.SemaphoreType.DMA
    nxt, spread = pl.pallas_call(
        kernel,
        out_shape=(
            jax.ShapeDtypeStruct((HALF, O * V), BF16),
            jax.ShapeDtypeStruct((8, 128), F32),
        ),
        in_specs=[hbm, hbm, hbm, hbm, vmem, smem, smem],
        out_specs=(vmem, vmem),
        scratch_shapes=[
            pltpu.VMEM((HALF, O * V), BF16),
            pltpu.VMEM((3 * O, 6 * O), BF16),
            pltpu.VMEM((2 * H, H), BF16),
            pltpu.VMEM((HALF, O * V), BF16),
            pltpu.VMEM((8, HALF, H), BF16),
            pltpu.VMEM((8, O, H), BF16),
            pltpu.VMEM((8, 2, 2, 4, O, H), BF16),
            pltpu.VMEM((16, 4, O, H), F32),
            pltpu.VMEM((16, 2, TILES, 8, 128), F32),
            pltpu.VMEM((16, 2, TILES, 8, 128), F32),
            pltpu.VMEM((16, 2, 2, TILES, 8, 128), F32),
            pltpu.VMEM((16, 2, 2, TILES, 8, 128), F32),
            pltpu.VMEM((8, 2, TILES, 8, 128), F32),
            pltpu.VMEM((8, 2, TILES, 8, 128), F32),
            pltpu.VMEM((8, 2, TILES, 8, 128), F32),
            pltpu.VMEM((16, TILES, 8, 128), F32),
            pltpu.VMEM((16, HALF, H), F32),
            pltpu.VMEM((2, 8, 128), F32),
            pltpu.VMEM((2, 8, 128), F32),
            pltpu.VMEM((3, 8, 128), F32),
            pltpu.VMEM((3, 3, 8, 128), F32),
            dma((4,)), dma((8,)), dma((8,)), dma((8,)), dma((8,)), dma((3, 8)),
            dma((len(SLOT),)), dma((8, 2)), dma((8, 2)), dma((8, 2)),
            dma((16, 2)), dma((16, 2)), dma((16, 2, 2)), dma((16, 2, 2)),
            dma((8,)), dma((8,)), dma((8, 2)), dma((16,)),
            dma((2,)), dma((2,)), dma((3, 3)), dma((3, 3)),
        ],
        compiler_params=pltpu.CompilerParams(
            collective_id=0, has_side_effects=True, vmem_limit_bytes=66 * 1024 * 1024 - 2 * 1024 * 1024 - 65536,
        ),
        name="sigma_step",
    )(r_vector, r_previous, cycle_block, weights, vir_energy, occ_energy, beta_previous)
    return (nxt, spread[0, :NVEC], spread[1, :NVEC])


def solution(mesh):
    placed = (
        P(("row", "col"), None),
        P(("row", "col"), None),
        P("row", "col"),
        P(None, "col", None, "row"),
        P(),
        P(),
        P(),
    )
    return jax.shard_map(
        on_device,
        mesh=mesh,
        in_specs=placed,
        out_specs=(P(("row", "col"), None), P(), P()),
        check_vma=False,
    )
```

```python
import functools

import jax
import jax.numpy as jnp
from jax import lax
from jax.experimental import pallas as pl
from jax.experimental.pallas import tpu as pltpu
from jax.sharding import PartitionSpec as P

O = 48
V = 384
NVEC = 64
COUNT = O * O * V
H = 1152
HALF = O // 2
MESH = pl.DeviceIdType.MESH
ORDER = ((0, 0), (0, 1), (0, 3), (1, 0), (0, 2), (1, 1), (1, 3), (1, 2))
FORWARD = {
    1: (("down", (0,), 4),),
    2: (("up", (1,), 4),),
    3: (("down", (0, 1), 5), ("up", (0, 1), 6)),
    5: (("down", (0,), 7),),
    6: (("up", (1,), 7),),
}
SLOT = {}
for _t in FORWARD:
    for _kind, _parts, _to in FORWARD[_t]:
        for _p in _parts:
            SLOT[(_t, _kind, _p)] = len(SLOT)
FIRST = (("down", 1), ("up", 2), ("across", 3))
F32 = jnp.float32
BF16 = jnp.bfloat16
HALVES = (
    (0, 0), (0, 1), (1, 0), (3, 0), (3, 1), (2, 0), (1, 1), (6, 0),
    (2, 1), (6, 1), (5, 0), (5, 1), (7, 0), (7, 1), (4, 0), (4, 1),
)
ARRIVALS = (
    (), (), ((3, 0), (1, 0),), (), ((2, 0), (1, 1), (3, 1), (2, 1),), (), ((6, 0), (5, 0),), (),
    ((4, 0),), ((6, 1),), ((5, 1),), (), ((7, 1), (4, 1), (7, 0),), (), (), (),
)
ROWS = HALF // 8
TILES = 6 * ROWS + 1
LEVELS = 43000.0
SPAN = 384.0
BIG = 12582912.0


def nearest(x):
    return (x + BIG) - BIG


def encode(src, dst):
    top = jnp.abs(src[:, 0:128])
    for k in range(1, H // 128):
        top = jnp.maximum(top, jnp.abs(src[:, k * 128:(k + 1) * 128]))
    peak = jnp.maximum(jnp.max(top), 1e-30)
    unit = jnp.full((8, 128), peak, F32) * (1.0 / LEVELS)
    dst[TILES - 1] = unit
    scale = 1.0 / unit
    for i in range(ROWS):
        rows = slice(i * 8, i * 8 + 8)
        for k in range(3):
            q = [nearest(src[rows, j * V + k * 128:j * V + k * 128 + 128] * scale) for j in range(3)]
            high = nearest(q[2] * (1.0 / 256.0))
            low = q[2] - high * 256.0
            dst[i * 3 + k] = q[0] * SPAN + high
            dst[3 * ROWS + i * 3 + k] = q[1] * SPAN + low


def decode_add(msgs, dst):
    units = [m[TILES - 1] for m in msgs]
    for i in range(ROWS):
        rows = slice(i * 8, i * 8 + 8)
        for k in range(3):
            at = [slice(j * V + k * 128, j * V + k * 128 + 128) for j in range(3)]
            total = [dst[rows, a] for a in at]
            for m, unit in zip(msgs, units):
                one, two = m[i * 3 + k], m[3 * ROWS + i * 3 + k]
                qa = nearest(one * (1.0 / SPAN))
                qb = nearest(two * (1.0 / SPAN))
                qc = (one - qa * SPAN) * 256.0 + (two - qb * SPAN)
                total = [t + v * unit for t, v in zip(total, (qa, qb, qc))]
            for a, t in zip(at, total):
                dst[rows, a] = t


def decode_set(msg, dst):
    unit = msg[TILES - 1]
    for i in range(ROWS):
        rows = slice(i * 8, i * 8 + 8)
        for k in range(3):
            one, two = msg[i * 3 + k], msg[3 * ROWS + i * 3 + k]
            qa = nearest(one * (1.0 / SPAN))
            qb = nearest(two * (1.0 / SPAN))
            qc = (one - qa * SPAN) * 256.0 + (two - qb * SPAN)
            for j, v in enumerate((qa, qb, qc)):
                dst[rows, j * V + k * 128:j * V + k * 128 + 128] = v * unit


def kernel(
    r_hbm, prev_hbm, c_hbm, w_hbm, vir_ref, occ_ref, bprev_ref,
    nxt_ref, g_ref,
    r_ref, w_ref, c_v, prev_v, sib, r48, ob, p, ao, ra, bo, tin, xo, xin, ho, hin, sig, st_out, st_in, g_out, g_in,
    load_sem, sib_s, sib_r, pa_s, pa_r, v_s, ag_s, ag_r, hs_s, hs_r,
    a_s, a_r, b_s, b_r, x_s, x_r, f_s, f_r, st_s, st_r, g_s, g_r,
):
    row, col = lax.axis_index("row"), lax.axis_index("col")
    xl, y = row // 4, row % 4
    xh, z, core = col // 8, (col % 8) // 2, col % 2

    def dev(xl_=None, y_=None, xh_=None, z_=None, core_=None):
        a = xl if xl_ is None else xl_
        b = y if y_ is None else y_
        c = xh if xh_ is None else xh_
        d = z if z_ is None else z_
        e = core if core_ is None else core_
        return (a * 4 + b, c * 8 + d * 2 + e)

    def remote(src, dst, ssem, rsem, to):
        return pltpu.make_async_remote_copy(
            src_ref=src, dst_ref=dst, send_sem=ssem, recv_sem=rsem,
            device_id=to, device_id_type=MESH,
        )

    y1, y2, y3 = (y + 1) % 4, (y + 2) % 4, (y + 3) % 4
    up, down = dev(z_=(z + 1) % 4), dev(z_=(z + 3) % 4)
    across = dev(xh_=1 - xh)
    sibling = dev(core_=1 - core)
    target = {"up": up, "down": down, "across": across}

    barrier = pltpu.get_barrier_semaphore()
    for d in range(1, 8):
        pl.semaphore_signal(barrier, inc=1, device_id=((row + d) % 8, col), device_id_type=MESH)
    for to in (sibling, up, down, across):
        pl.semaphore_signal(barrier, inc=1, device_id=to, device_id_type=MESH)
    load_r = pltpu.make_async_copy(r_hbm, r_ref, load_sem.at[2])
    load_w = pltpu.make_async_copy(w_hbm, w_ref, load_sem.at[3])
    load_r.start()
    load_c = pltpu.make_async_copy(c_hbm, c_v, load_sem.at[0])
    load_p = pltpu.make_async_copy(prev_hbm, prev_v, load_sem.at[1])
    load_c.start()
    load_p.start()
    load_w.start()
    load_r.wait()
    pl.semaphore_wait(barrier, 11)

    def rel(d):
        yd, xd = (y + d % 4) % 4, (xl + d // 4) % 2
        return yd, xd

    def cols(yd, xd, half):
        return pl.ds(pl.multiple_of(((xd * 4 + yd) * 2 + half) * H, 128), H)

    near, far = (1, 3, 2), (4, 5, 7, 6)

    def swap(d):
        yd, xd = rel(d)
        return remote(r_ref.at[:, cols(yd, xd, 1 - core)], sib.at[d], sib_s.at[d], sib_r.at[d], sibling)

    blk0 = xh * 4 + z

    def exchange(d):
        yd, xd = rel(d)
        return remote(r48.at[d], ob.at[blk0, core, xl, y], pa_s.at[d], pa_r.at[d], dev(xl_=xd, y_=yd))

    def pass_on(d, to):
        kind, block = FIRST[to]
        ys, xs = (y + 4 - d % 4) % 4, (xl + d // 4) % 2
        piece = ob.at[blk0, core, xs, ys]
        return remote(piece, piece, v_s.at[to, d], ag_r.at[block, d // 4], target[kind])

    for d in (0,) + near + far:
        swap(d).start()
    def prepare(d):
        yd, xd = rel(d)
        swap(d).wait_recv()
        mine = r_ref[:, cols(yd, xd, core)].astype(F32)
        other = sib[d].astype(F32)
        first = jnp.where(core == 0, mine, other)
        second = jnp.where(core == 0, other, mine)
        both = jnp.concatenate([first, second], axis=0).astype(BF16)
        if d == 0:
            ob[blk0, core, xl, y] = both
        else:
            r48[d] = both
            exchange(d).start()

    for d in (0, 2, 1, 3, 6, 5, 7, 4):
        prepare(d)
    for to in range(3):
        pass_on(0, to).start()
    for d in near:
        exchange(d).wait_recv()
        for to in range(3):
            pass_on(d, to).start()

    def block_of(t):
        out_x, out_z = xh, z
        for k, (dx, dz) in enumerate(ORDER):
            out_x = jnp.where(t == k, (xh + dx) % 2, out_x)
            out_z = jnp.where(t == k, (z + dz) % 4, out_z)
        return out_x, out_z

    def forward(t, kind, part, to):
        dx, dz = ORDER[t]
        blk = ((xh + dx) % 2) * 4 + (z + dz) % 4
        piece = ob.at[blk, core, (part + xl) % 2]
        return remote(piece, piece, ag_s.at[SLOT[(t, kind, part)]], ag_r.at[to, part], target[kind])

    def hand(t, part):
        bx, bz = block_of(t)
        piece = ob.at[bx * 4 + bz, core, (part + xl) % 2]
        return remote(piece, piece, hs_s.at[t, part], hs_r.at[t, part], sibling)

    def landed(t, part):
        bx, bz = block_of(t)
        piece = ob.at[bx * 4 + bz, core, (part + xl) % 2]
        return remote(piece, piece, ag_s.at[0], ag_r.at[t, part], sibling)

    def sibling_landed(t, part):
        bx, bz = block_of(t)
        piece = ob.at[bx * 4 + bz, 1 - core, (part + xl) % 2]
        return remote(piece, piece, hs_s.at[t, part], hs_r.at[t, part], sibling)

    def half_of(u):
        t, g, keep = jnp.int32(0), jnp.int32(0), jnp.int32(0)
        for k, (bt, bg) in enumerate(HALVES):
            t, g = jnp.where(u == k, bt, t), jnp.where(u == k, bg, g)
            keep = jnp.where(u == k, HALVES.index((bt, 0)), keep)
        return t, g, keep

    def first_hop(s, side):
        to = dev(y_=y1) if side == 0 else dev(y_=y3)
        return remote(ao.at[s, side], ra.at[s, side], a_s.at[s, side], a_r.at[s, side], to)

    def second_hop(s, side, which):
        yd = y1 if side == 0 else y3
        return remote(
            bo.at[s, side, which], tin.at[s, side, which],
            b_s.at[s, side, which], b_r.at[s, side, which], dev(y_=yd),
        )

    def beside(t):
        return remote(xo.at[t], xin.at[t], x_s.at[t], x_r.at[t], dev(xl_=1 - xl))

    def home(t, core_to):
        bx, bz = block_of(t)
        return remote(
            ho.at[t, core_to], hin.at[col], f_s.at[t, core_to], f_r.at[col],
            dev(xh_=bx, z_=bz, core_=core_to),
        )

    def home_sibling():
        return remote(ho.at[0, 0], hin.at[col], f_s.at[0, 0], f_r.at[col], sibling)

    load_c.wait()
    load_w.wait()

    rows_of = (slice(0, HALF), slice(HALF, O))

    def relay(u):
        for side in range(2):
            first_hop(u, side).wait_recv()
            share = p.at[u, y1 if side == 0 else y3, rows_of[side]]
            decode_add([ra.at[u, side]], share)
            encode(share, bo.at[u, side, side])
            second_hop(u, side, side).start()

    def across_pair(u):
        t, g, _ = half_of(u)
        for which in range(2):
            second_hop(u, 0, which).wait_recv()
            second_hop(u, 1, which).wait_recv()
            decode_add([tin.at[u, 0, which], tin.at[u, 1, which]], p.at[u, y, rows_of[which]])

        @pl.when(g == 1)
        def _():
            for which in range(2):
                encode(p.at[u, y, rows_of[which]], xo.at[t, which])
            beside(t).start()

    def deliver(u):
        t, g, keep = half_of(u)

        @pl.when(g == 1)
        def _():
            beside(t).wait_recv()
            for which in range(2):
                decode_add([xin.at[t, which]], p.at[keep, y, rows_of[which]])

            @pl.when(t == 0)
            def _():
                encode(p.at[0, y, pl.ds(pl.multiple_of((1 - core) * HALF, 8), HALF)], ho.at[0, 0])
                home_sibling().start()
                sig[col] = p[0, y, pl.ds(pl.multiple_of(core * HALF, 8), HALF)]

            @pl.when(t > 0)
            def _():
                for which in range(2):
                    encode(p.at[keep, y, rows_of[which]], ho.at[t, which])
                    home(t, which).start()

    def step(u, carry):
        t, g, _ = half_of(u)

        @pl.when(u < 2)
        def _():
            hand(0, u).start()

        for k, todo in enumerate(ARRIVALS):
            if todo:
                @pl.when(u == k)
                def _(todo=todo):
                    for bt, part in todo:
                        landed(bt, part).wait_recv()
                        for kind, parts, to in FORWARD.get(bt, ()):
                            if part in parts:
                                forward(bt, kind, part, to).start()
                        hand(bt, part).start()

        @pl.when(u < 16)
        def _():
            sibling_landed(t, g).wait_recv()
            bx, bz = block_of(t)
            h = (g + xl) % 2
            blk = bx * 4 + bz
            x0 = ob[blk, 0, h].reshape(4 * O, H)
            x1 = ob[blk, 1, h].reshape(4 * O, H)
            acc = jnp.dot(x0, c_v[:H], preferred_element_type=F32)
            acc = acc + jnp.dot(x1, c_v[H:], preferred_element_type=F32)
            p[u] = acc.reshape(4, O, H)

            def ladder(v, carry2):
                stack = jnp.concatenate(
                    [ob[blk, w, h, v, :, q * V:(q + 1) * V] for w in range(2) for q in range(3)],
                    axis=0,
                )
                part = jnp.dot(w_ref[...], stack, preferred_element_type=F32)
                for j in range(3):
                    p[u, v, :, j * V:(j + 1) * V] += part[j * O:(j + 1) * O]
                return carry2

            @pl.when(u == 0)
            def _():
                for d in far:
                    exchange(d).wait_recv()
                    for to in range(3):
                        pass_on(d, to).start()

            ladder(y2, 0)
            for side in range(2):
                encode(p.at[u, y2, rows_of[side]], ao.at[u, side])
                first_hop(u, side).start()
            for side in range(2):
                yd = y1 if side == 0 else y3
                ladder(yd, 0)
                encode(p.at[u, yd, rows_of[1 - side]], bo.at[u, side, 1 - side])
                second_hop(u, side, 1 - side).start()
            ladder(y, 0)

        @pl.when(jnp.logical_and(u >= 1, u <= 16))
        def _():
            relay(u - 1)

        @pl.when(jnp.logical_and(u >= 3, u <= 18))
        def _():
            across_pair(u - 3)

        @pl.when(u >= 4)
        def _():
            deliver(u - 4)

        return carry

    lax.fori_loop(0, 20, step, 0)
    load_p.wait()

    def sums(val):
        total = val[:, 0:128]
        for k in range(1, H // 128):
            total = total + val[:, k * 128:(k + 1) * 128]
        return total[0:8] + total[8:16] + total[16:24]

    line24 = lax.broadcasted_iota(jnp.int32, (HALF, 128), 0)
    occ_mat = jnp.zeros((HALF, 128), F32)
    for i in range(HALF):
        occ_mat = jnp.where(line24 == i, occ_ref[core * HALF + i], occ_mat)
    occ_col = occ_mat[:, 0:1]
    vir_row = vir_ref[...].reshape(1, V)

    def arrived(d):
        from_col = (col + d) % 16
        return remote(ho.at[0, 0], hin.at[from_col], f_s.at[0, 0], f_r.at[from_col], sibling)

    def first_pass(d, carry):
        acc_s, acc_r = carry
        @pl.when(d > 0)
        def _():
            arrived(d).wait_recv()
            decode_set(hin.at[(col + d) % 16], sig.at[(col + d) % 16])
        k = (col + d) % 16
        rv = r_ref[:, pl.ds(pl.multiple_of(k * H, 128), H)].astype(F32)
        levels = jnp.concatenate([vir_row - occ_ref[k * 3 + j] for j in range(3)], axis=1)
        val = sig[k] + (levels - occ_col) * rv
        sig[k] = val
        return acc_s + sums(rv * val), acc_r + sums(rv * rv)

    zero = jnp.zeros((8, 128), F32)
    acc_s, acc_r = lax.fori_loop(0, 16, first_pass, (zero, zero))
    line = lax.broadcasted_iota(jnp.int32, (8, 128), 0)

    def pair(k):
        return remote(st_out.at[k], st_in.at[k], st_s.at[k], st_r.at[k], sibling)

    st_out[0] = jnp.where(line == 0, jnp.sum(acc_s), jnp.sum(acc_r))
    pair(0).start()
    pair(0).wait_recv()
    both = st_out[0] + st_in[0]
    alpha = both[0:1] / COUNT / (both[1:2] / COUNT + 1e-06)
    alpha_1 = alpha[:, 0:1]
    bprev_1 = bprev_ref[row * 8 + xh * 4 + z]

    def second_pass(k, acc):
        at = pl.ds(pl.multiple_of(k * H, 128), H)
        val = sig[k] - alpha_1 * r_ref[:, at].astype(F32) - bprev_1 * prev_v[:, at].astype(F32)
        sig[k] = val
        return acc + sums(val * val)

    acc_n = lax.fori_loop(0, 16, second_pass, zero)
    st_out[1] = jnp.where(line == 0, jnp.sum(acc_n), 0.0)
    pair(1).start()
    pair(1).wait_recv()
    norm = (st_out[1] + st_in[1])[0:1]
    beta = jnp.sqrt(norm / COUNT + 1e-06)
    inv = (1.0 / beta)[:, 0:1]

    lane = lax.broadcasted_iota(jnp.int32, (8, 128), 1)
    vec = row * 8 + xh * 4 + z
    g_out[0] = jnp.where(lane == vec, jnp.where(line == 0, alpha, beta), 0.0)

    def spread(axis, d):
        if axis == 0:
            to = dev(z_=(z + d) % 4)
        elif axis == 1:
            to = dev(y_=(y + d) % 4)
        else:
            to = dev(xl_=(xl + d % 2) % 2, xh_=(xh + d // 2) % 2)
        return remote(g_out.at[axis], g_in.at[axis, d - 1], g_s.at[axis, d - 1], g_r.at[axis, d - 1], to)

    for d in range(1, 4):
        spread(0, d).start()

    def third_pass(k, carry):
        nxt_ref[:, pl.ds(pl.multiple_of(k * H, 128), H)] = (sig[k] * inv).astype(BF16)
        return carry

    lax.fori_loop(0, 16, third_pass, 0)
    for axis in range(3):
        for d in range(1, 4):
            spread(axis, d).wait_recv()
        merged = g_out[axis] + g_in[axis, 0] + g_in[axis, 1] + g_in[axis, 2]
        if axis == 2:
            g_ref[...] = merged
        else:
            g_out[axis + 1] = merged
            for d in range(1, 4):
                spread(axis + 1, d).start()

    for d in range(8):
        swap(d).wait_send()
        if d:
            exchange(d).wait_send()
        for to in range(3):
            pass_on(d, to).wait_send()
    for bt in FORWARD:
        for kind, parts, to in FORWARD[bt]:
            for part in parts:
                forward(bt, kind, part, to).wait_send()

    def drain(u, carry):
        t, g, keep = half_of(u)
        hand(t, g).wait_send()
        for side in range(2):
            first_hop(u, side).wait_send()
            second_hop(u, side, 0).wait_send()
            second_hop(u, side, 1).wait_send()

        @pl.when(g == 1)
        def _():
            beside(t).wait_send()

            @pl.when(t == 0)
            def _():
                home_sibling().wait_send()

            @pl.when(t > 0)
            def _():
                home(t, 0).wait_send()
                home(t, 1).wait_send()

        return carry

    lax.fori_loop(0, 16, drain, 0)
    pair(0).wait_send()
    pair(1).wait_send()
    for axis in range(3):
        for d in range(1, 4):
            spread(axis, d).wait_send()


def on_device(
    r_vector, r_previous, cycle_block, ladder_block, occ_energy, vir_energy, beta_previous
):
    weights = jnp.transpose(ladder_block, (1, 0, 3, 2)).reshape(3 * O, 6 * O)
    vmem, hbm = pl.BlockSpec(memory_space=pltpu.VMEM), pl.BlockSpec(memory_space=pl.ANY)
    smem = pl.BlockSpec(memory_space=pltpu.SMEM)
    dma = pltpu.SemaphoreType.DMA
    nxt, spread = pl.pallas_call(
        kernel,
        out_shape=(
            jax.ShapeDtypeStruct((HALF, O * V), BF16),
            jax.ShapeDtypeStruct((8, 128), F32),
        ),
        in_specs=[hbm, hbm, hbm, hbm, vmem, smem, smem],
        out_specs=(vmem, vmem),
        scratch_shapes=[
            pltpu.VMEM((HALF, O * V), BF16),
            pltpu.VMEM((3 * O, 6 * O), BF16),
            pltpu.VMEM((2 * H, H), BF16),
            pltpu.VMEM((HALF, O * V), BF16),
            pltpu.VMEM((8, HALF, H), BF16),
            pltpu.VMEM((8, O, H), BF16),
            pltpu.VMEM((8, 2, 2, 4, O, H), BF16),
            pltpu.VMEM((16, 4, O, H), F32),
            pltpu.VMEM((16, 2, TILES, 8, 128), F32),
            pltpu.VMEM((16, 2, TILES, 8, 128), F32),
            pltpu.VMEM((16, 2, 2, TILES, 8, 128), F32),
            pltpu.VMEM((16, 2, 2, TILES, 8, 128), F32),
            pltpu.VMEM((8, 2, TILES, 8, 128), F32),
            pltpu.VMEM((8, 2, TILES, 8, 128), F32),
            pltpu.VMEM((8, 2, TILES, 8, 128), F32),
            pltpu.VMEM((16, TILES, 8, 128), F32),
            pltpu.VMEM((16, HALF, H), F32),
            pltpu.VMEM((2, 8, 128), F32),
            pltpu.VMEM((2, 8, 128), F32),
            pltpu.VMEM((3, 8, 128), F32),
            pltpu.VMEM((3, 3, 8, 128), F32),
            dma((4,)), dma((8,)), dma((8,)), dma((8,)), dma((8,)), dma((3, 8)),
            dma((len(SLOT),)), dma((8, 2)), dma((8, 2)), dma((8, 2)),
            dma((16, 2)), dma((16, 2)), dma((16, 2, 2)), dma((16, 2, 2)),
            dma((8,)), dma((8,)), dma((8, 2)), dma((16,)),
            dma((2,)), dma((2,)), dma((3, 3)), dma((3, 3)),
        ],
        compiler_params=pltpu.CompilerParams(
            collective_id=0, has_side_effects=True, vmem_limit_bytes=66 * 1024 * 1024 - 2 * 1024 * 1024 - 65536,
        ),
        name="sigma_step",
    )(r_vector, r_previous, cycle_block, weights, vir_energy, occ_energy, beta_previous)
    return (nxt, spread[0, :NVEC], spread[1, :NVEC])


def solution(mesh):
    placed = (
        P(("row", "col"), None),
        P(("row", "col"), None),
        P("row", "col"),
        P(None, "col", None, "row"),
        P(),
        P(),
        P(),
    )
    return jax.shard_map(
        on_device,
        mesh=mesh,
        in_specs=placed,
        out_specs=(P(("row", "col"), None), P(), P()),
        check_vma=False,
    )
```
